32 devices in a mesh: band: 8 (over z, y), mode: 4 (over x, core).
Axes of the slice: x: 2, y: 2, z: 4, core: 2. Of those that a mesh axis runs over, the one named last changes fastest.
Arguments:
- velocity: bfloat16 [1, 8192, 1024], P(None, ('band', 'mode')), may hold values from -6 to 6
- radiation_modes: bfloat16 [8192, 1024], P('band', 'mode'), may hold values from -0.125 to 0.125
- resistance: float32 [8, 1024, 1024], P('band', None, 'mode'), as said below
- mode_ranks: int32 [8], P('band'), may hold values from 128 to 1024, as said below
- freq_table: int32 [512], replicated, may hold values from 0 to 511, each once
Outputs:
- adjoint_force: bfloat16 [1, 8192, 1024], P(None, ('band', 'mode'))
The draws below stay inside these ranges and needn't reach their ends.
Inputs may be any that keep to these rules, and one draw needn't show every extreme that they name: `resistance`: each band's matrix is symmetric. `mode_ranks`: the ranks never fall with the band index; the first band keeps 1024 // 8 modes and the last 1024.
All inputs are finite; a program needn't handle non-finite values.
Results may differ from the reference program's by a relative error of at most 0.015.
Values may be sent and summed in bfloat16 or wider, within the bound.
A program may use at most 64 MiB of HBM per device.

```python
import math
import jax
import jax.numpy as jnp
from jax import lax

WIN = 1
NT = 1024
F = 512
RMAX = 1024
PATCHES = 8192
NBANDS = 8
FPB = 64


def draw_resistance(key, part):
    first_key, second_key = jax.random.split(jax.random.fold_in(key, 11))
    noise = jax.random.normal(first_key, (NBANDS, RMAX, RMAX), jnp.float32)
    symmetric = (noise + jnp.swapaxes(noise, 1, 2)) * (0.5 / jnp.sqrt(jnp.float32(RMAX)))
    diagonal_part = jax.random.uniform(second_key, (NBANDS, RMAX), jnp.float32, 0.5, 2.0)
    identity = jnp.eye(RMAX, dtype=jnp.float32)
    return symmetric + diagonal_part[:, :, None] * identity[None, :, :]


def draw_mode_ranks(key, part):
    drawn = jax.random.randint(jax.random.fold_in(key, 23), (NBANDS,), RMAX // 8, RMAX + 1, jnp.int32)
    ordered = jnp.sort(drawn)
    ordered = ordered.at[0].set(RMAX // 8)
    ordered = ordered.at[NBANDS - 1].set(RMAX)
    return ordered.astype(jnp.int32)


def level_of(key, extent, cuts, least, top_value):
    def one(dim, parts):
        steps = jax.random.uniform(jax.random.fold_in(jax.random.fold_in(key, 6), dim), (parts,), jnp.float32, least / len(cuts), top_value / len(cuts))
        return jnp.repeat(jnp.exp(steps), extent[dim] // parts).reshape((-1,) + (1,) * (len(extent) - dim - 1))

    factor_of = one(*cuts[0])
    for cut in cuts[1:]:
        factor_of = factor_of * one(*cut)
    return factor_of


def normal_values(key, dims, scale, limit, cuts=(), kind=jnp.bfloat16):
    values = jax.random.normal(key, dims, jnp.float32) * scale
    if len(cuts) > 0:
        values = level_of(key, dims, cuts, -0.22, 0.18) * values
    return jnp.clip(values, min=-limit, max=limit).astype(kind)


def setup_inputs(seed: int = 0) -> dict:
    keys = jax.random.split(jax.random.key(seed), 6)
    velocity = normal_values(keys[0], (WIN, PATCHES, NT), 1.0, 6.0, ((1, 32),))
    radiation_modes = normal_values(keys[1], (PATCHES, RMAX), (PATCHES // 4) ** -0.5, 0.125, ((0, 8), (1, 4)))
    resistance = draw_resistance(jax.random.fold_in(keys[5], 71), 0)
    mode_ranks = draw_mode_ranks(jax.random.fold_in(keys[5], 71), 0)
    freq_table = jax.random.permutation(keys[4], F).astype(jnp.int32)
    return {"velocity": velocity, "radiation_modes": radiation_modes, "resistance": resistance, "mode_ranks": mode_ranks, "freq_table": freq_table}


def make_table(freq_table):
    times = jnp.arange(NT, dtype=jnp.int32)
    phases = times[:, None] * freq_table[None, :].astype(jnp.int32) % NT
    angles = phases.astype(jnp.float32) * (2.0 * math.pi / NT)
    norming = 1.0 / math.sqrt(NT)
    table = jnp.stack([jnp.cos(angles), -jnp.sin(angles)], axis=1) * norming
    return table.astype(jnp.bfloat16)

def reference(velocity, radiation_modes, resistance, mode_ranks, freq_table):
    table_wide = make_table(freq_table).astype(jnp.float32)
    modes_wide = radiation_modes.astype(jnp.float32)
    rank_mask = (jnp.arange(RMAX, dtype=jnp.int32)[:, None] < mode_ranks[None, :]).astype(jnp.float32)
    rank_mask = rank_mask[:, None, :, None]
    results = []
    for window in range(WIN):
        spectra = jnp.einsum('pt,tcf->pcf', velocity[window].astype(jnp.float32), table_wide).astype(jnp.bfloat16)
        coefficients = jnp.einsum('pr,pcf->rcf', modes_wide, spectra.astype(jnp.float32))
        coefficients = coefficients.reshape(RMAX, 2, NBANDS, FPB) * rank_mask
        forcing = jnp.einsum('bij,jcbf->icbf', resistance, coefficients, precision=lax.Precision.HIGHEST)
        forcing = (2.0 * forcing * rank_mask).astype(jnp.bfloat16).reshape(RMAX, 2, F)
        surface_force = jnp.einsum('pr,rcf->pcf', modes_wide, forcing.astype(jnp.float32)).astype(jnp.bfloat16)
        history = jnp.einsum('pcf,tcf->pt', surface_force.astype(jnp.float32), table_wide)
        results.append(history.astype(jnp.bfloat16))
    return jnp.stack(results, axis=0)
```

```python
import functools
import math

import jax
import jax.numpy as jnp
from jax import lax
from jax.experimental import pallas as pl
from jax.experimental.pallas import tpu as pltpu
from jax.sharding import PartitionSpec as P

MESH = pl.DeviceIdType.MESH
HALF_ROWS = 32


def cosine_of(phase, period):
    wrapped = phase & (period - 1)
    folded = jnp.minimum(wrapped, period - wrapped)
    flip = folded > period // 4
    folded = jnp.where(flip, period // 2 - folded, folded)
    x = folded.astype(jnp.float32) * (2.0 * math.pi / period)
    y = x * x
    value = jnp.full_like(y, 1.0 / math.factorial(16))
    for n in range(14, -1, -2):
        sign = -1.0 if n % 4 else 1.0
        value = value * y + sign / math.factorial(n)
    return jnp.where(flip, -value, value)


def fused_kernel(
    nb, nm, vel_hbm, modes_hbm, res_hbm, rank_hbm, freq_hbm, out_ref,
    vel_ref, modes_ref, res_ref, rank_ref, freq_ref,
    table, trig, modes_t, res_hi, res_lo, spec, part, pend, rs, coef, force, basis, acc,
    in_s, sx_s, sx_r, sm_s, sm_r, sf_s, sf_r, ry_s, ry_r, rs_s, rs_r, k_s, k_r, ob_s, ob_r,
    fz_s, fz_r, fy_s, fy_r, fx_s, fx_r, gy_s, gy_r, gx_s, gx_r, fm_s, fm_r, ff_s, ff_r,
):
    b = lax.axis_index("band")
    m = lax.axis_index("mode")
    mate = m + 1 - 2 * (m % 2)
    cross = (m + 2) % nm
    diag = (mate + 2) % nm
    patches, steps = vel_ref.shape
    cols = table.shape[2]
    mode_cols = modes_ref.shape[1]

    def band_at(e):
        bits = [1 << i for i in range(nb.bit_length() - 1)]
        return sum(bit * ((b // bit + e // bit) % 2) for bit in bits)

    def to_mode(src, dst, send, recv, target):
        return pltpu.make_async_remote_copy(
            src_ref=src, dst_ref=dst, send_sem=send, recv_sem=recv,
            device_id={"mode": target}, device_id_type=MESH)

    def to_band(src, dst, send, recv, target):
        return pltpu.make_async_remote_copy(
            src_ref=src, dst_ref=dst, send_sem=send, recv_sem=recv,
            device_id={"band": target}, device_id_type=MESH)

    loads = [
        pltpu.make_async_copy(src, dst, in_s.at[i])
        for i, (src, dst) in enumerate((
            (freq_hbm, freq_ref), (vel_hbm, vel_ref), (modes_hbm, modes_ref),
            (res_hbm, res_ref), (rank_hbm, rank_ref)))
    ]
    for load in loads:
        load.start()
    barrier = pltpu.get_barrier_semaphore()
    for off in range(1, nm):
        pl.semaphore_signal(barrier, inc=1, device_id={"mode": (m + off) % nm}, device_id_type=MESH)
    for off in range(1, nb):
        pl.semaphore_signal(barrier, inc=1, device_id={"band": band_at(off)}, device_id_type=MESH)

    blocks = steps // HALF_ROWS
    norming = 1.0 / math.sqrt(steps)

    def build(k):
        half = cols // 2
        lane = lax.broadcasted_iota(jnp.int32, (HALF_ROWS, cols), 1)
        row = jnp.broadcast_to(freq_ref[pl.ds(k // 2, 1), :], (HALF_ROWS, cols))
        freq = jnp.where(lane // half == k % 2, row, pltpu.roll(row, half, 1))
        shift = jnp.where(lane < half, 0, steps // 4)
        rows = lax.broadcasted_iota(jnp.int32, (HALF_ROWS, cols), 0)
        big = lax.broadcasted_iota(jnp.int32, (blocks, cols), 0) * HALF_ROWS
        low = rows * freq + shift
        high = big * freq
        quarter = steps // 4
        cos_low = cosine_of(low, steps) * norming
        sin_low = cosine_of(low - quarter, steps) * norming
        trig[0] = cosine_of(high, steps)
        trig[1] = cosine_of(high - quarter, steps)
        for a in range(blocks):
            row = trig[0, pl.ds(a, 1), :] * cos_low - trig[1, pl.ds(a, 1), :] * sin_low
            table[k, pl.ds(a * HALF_ROWS, HALF_ROWS), :] = row.astype(jnp.bfloat16)

    def project(k):
        spec[k, m] = jnp.dot(
            vel_ref[...], table[k], preferred_element_type=jnp.float32
        ).astype(jnp.bfloat16)

    loads[0].wait()
    build(band_at(nb - 1))
    loads[1].wait()
    project(band_at(nb - 1))
    pl.semaphore_wait(barrier, nm - 1 + nb - 1)

    def s_cross(k):
        return to_mode(spec.at[k, m], spec.at[k, m], sx_s.at[k], sx_r.at[k], cross)

    def s_mate(k):
        return to_mode(spec.at[k, m], spec.at[k, m], sm_s.at[k], sm_r.at[k], mate)

    def s_fwd(k):
        return to_mode(spec.at[k, cross], spec.at[k, cross], sf_s.at[k], sf_r.at[k], mate)

    def spec_step(i, _):
        k = band_at(nb - 1 - i)
        s_cross(k).start()
        s_mate(k).start()
        build(band_at(nb - 2 - i))
        project(band_at(nb - 2 - i))
        return 0

    lax.fori_loop(0, nb - 1, spec_step, 0)
    s_cross(b).start()
    s_mate(b).start()

    def basis_copy(off):
        target = (m + off) % nm
        rows = pl.ds(pl.multiple_of(target * patches, patches), patches)
        return to_mode(modes_ref.at[rows], basis.at[m], ob_s.at[off], ob_r.at[off], target)

    loads[2].wait()
    for off in range(1, nm):
        basis_copy(off).start()
    modes_t[...] = modes_ref[...].T
    loads[3].wait()
    wide = res_ref[...].T
    narrow = wide.astype(jnp.bfloat16)
    res_hi[...] = narrow
    res_lo[...] = (wide - narrow.astype(jnp.float32)).astype(jnp.bfloat16)
    loads[4].wait()

    def partial(k):
        return jnp.dot(
            modes_t[...], spec[k].reshape(nm * patches, cols), preferred_element_type=jnp.float32)

    near = band_at(1)
    pairs = nb // 2

    def y_copy(j):
        k = band_at(2 * j + 1)
        return to_band(part.at[k], rs.at[j], ry_s.at[j], ry_r.at[j], near)

    def z_copy(j):
        k = band_at(2 * j)
        return to_band(part.at[k], rs.at[pairs + j], rs_s.at[j], rs_r.at[j], k)

    def gather(k):
        s_cross(k).wait_recv()
        s_fwd(k).start()
        s_mate(k).wait_recv()
        s_fwd(k).wait_recv()
        return partial(k)

    def away(j):
        k = band_at(2 * j + 1)
        part[k] = gather(k).astype(jnp.bfloat16)
        y_copy(j).start()

    def pass_on(j):
        y_copy(j).wait_recv()
        part[band_at(2 * j)] = (pend[...] + rs[j].astype(jnp.float32)).astype(jnp.bfloat16)
        z_copy(j).start()

    away(pairs - 1)
    pend[...] = gather(band_at(nb - 2))

    def part_step(i, _):
        j = pairs - 2 - i
        away(j)
        pass_on(j + 1)
        pend[...] = gather(band_at(2 * j))
        return 0

    lax.fori_loop(0, pairs - 1, part_step, 0)
    total = pend[...]
    for j in range(pairs - 1, 0, -1):
        z_copy(j).wait_recv()
        total = total + rs[pairs + j].astype(jnp.float32)
    y_copy(0).wait_recv()
    total = total + rs[0].astype(jnp.float32)
    kept = lax.broadcasted_iota(jnp.int32, (mode_cols, cols), 0) + m * mode_cols < rank_ref[...]
    total = jnp.where(kept, total, 0.0)
    coef[m] = total.astype(jnp.bfloat16)

    def k_copy(off):
        return to_mode(coef.at[m], coef.at[m], k_s.at[off], k_r.at[off], (m + off) % nm)

    def k_arrival(off):
        source = (m + nm - off) % nm
        return to_mode(coef.at[source], coef.at[source], k_s.at[off], k_r.at[off], source)

    for off in range(1, nm):
        k_copy(off).start()
    for off in range(1, nm):
        k_arrival(off).wait_recv()
    coefs = coef[...].reshape(nm * mode_cols, cols)
    forcing = jnp.dot(res_hi[...], coefs, preferred_element_type=jnp.float32) + jnp.dot(
        res_lo[...], coefs, preferred_element_type=jnp.float32)
    forcing = jnp.where(kept, 2.0 * forcing, 0.0)
    force[b, m] = forcing.astype(jnp.bfloat16)

    half = mode_cols // 2
    upper, lower = pl.ds(0, half), pl.ds(half, half)

    def f_far(k):
        return to_band(force.at[b, m], force.at[b, m], fz_s.at[k], fz_r.at[b], k)

    def f_far_arrival(k):
        return to_band(force.at[k, m], force.at[k, m], fz_s.at[k], fz_r.at[k], k)

    def f_near(k):
        return to_band(force.at[k, m], force.at[k, m], fy_s.at[k], fy_r.at[k], near)

    def f_cross(k):
        return to_mode(force.at[k, m], force.at[k, m], fx_s.at[k], fx_r.at[k], cross)

    def g_near(k):
        piece = force.at[k, cross, lower]
        return to_band(piece, piece, gy_s.at[k], gy_r.at[k], near)

    def g_cross(k):
        piece = force.at[k, m, upper]
        return to_mode(piece, piece, gx_s.at[k], gx_r.at[k], cross)

    def f_mate(k):
        return to_mode(force.at[k, m], force.at[k, m], fm_s.at[k], fm_r.at[k], mate)

    def f_fwd(k):
        return to_mode(force.at[k, cross], force.at[k, cross], ff_s.at[k], ff_r.at[k], mate)

    far = list(range(0, nb, 2))

    def first(j):
        k = band_at(far[j])
        if j > 0:
            f_far_arrival(k).wait_recv()
        f_near(k).start()
        f_cross(k).start()
        f_mate(k).start()

    def second(j):
        k, k1 = band_at(far[j]), band_at(far[j] + 1)
        f_near(k1).wait_recv()
        g_cross(k1).start()
        f_mate(k1).start()
        f_cross(k).wait_recv()
        g_near(k).start()
        f_fwd(k).start()

    def third(j):
        k1 = band_at(far[j] + 1)
        g_cross(k1).wait_recv()
        g_near(k1).wait_recv()
        f_fwd(k1).start()

    for e in far[1:]:
        f_far(band_at(e)).start()
    first(0)

    for off in range(1, nm):
        source = (m + nm - off) % nm
        to_mode(basis.at[source], basis.at[source], ob_s.at[off], ob_r.at[off], source).wait_recv()
    basis[m] = modes_ref[pl.ds(pl.multiple_of(m * patches, patches), patches), :]

    def surface(k):
        value = jnp.dot(basis[0], force[k, 0], preferred_element_type=jnp.float32)
        for j in range(1, nm):
            value = value + jnp.dot(basis[j], force[k, j], preferred_element_type=jnp.float32)
        return value.astype(jnp.bfloat16)

    def history(k):
        f_mate(k).wait_recv()
        f_fwd(k).wait_recv()
        return lax.dot_general(
            surface(k), table[k], (((1,), (1,)), ((), ())), preferred_element_type=jnp.float32)

    def last(e):
        term = history(band_at(e))
        if e == 0:
            acc[...] = term
        elif e < nb - 1:
            acc[...] += term
        else:
            out_ref[...] = (acc[...] + term).astype(out_ref.dtype)

    n = len(far)
    for j in range(1, n):
        first(j)
    for j in range(n):
        second(j)
    last(0)
    third(0)
    for j in range(1, n):
        last(far[j])
        if j > 1:
            last(far[j] - 3)
        third(j)
    last(far[n - 1] - 1)
    last(far[n - 1] + 1)

    def drain(k, _):
        for copy in (s_cross, s_mate, s_fwd, f_mate, f_fwd):
            copy(k).wait_send()
        return 0

    lax.fori_loop(0, nb, drain, 0)
    for j in range(pairs):
        y_copy(j).wait_send()
        if j > 0:
            z_copy(j).wait_send()
    for e in far:
        k, k1 = band_at(e), band_at(e + 1)
        if e > 0:
            f_far(k).wait_send()
        f_near(k).wait_send()
        f_cross(k).wait_send()
        g_near(k).wait_send()
        g_cross(k1).wait_send()
    for off in range(1, nm):
        basis_copy(off).wait_send()
        k_copy(off).wait_send()


def fused(mesh, velocity, radiation_modes, resistance, mode_ranks, freq_table):
    nb, nm = mesh.shape["band"], mesh.shape["mode"]
    patches, steps = velocity.shape[1:]
    mode_cols = radiation_modes.shape[1]
    modes = nm * mode_cols
    cols = 2 * (freq_table.shape[0] // nb)
    bf16, f32 = jnp.bfloat16, jnp.float32
    dma = lambda n: pltpu.SemaphoreType.DMA((n,))
    vmem = pl.BlockSpec(memory_space=pltpu.VMEM)
    hbm = pl.BlockSpec(memory_space=pltpu.HBM)
    out = pl.pallas_call(
        functools.partial(fused_kernel, nb, nm),
        out_shape=pltpu.VMEM((patches, steps), bf16),
        in_specs=[hbm] * 5,
        out_specs=vmem,
        scratch_shapes=[
            pltpu.VMEM((patches, steps), bf16),
            pltpu.VMEM(radiation_modes.shape, bf16),
            pltpu.VMEM(resistance.shape[1:], f32),
            pltpu.VMEM((1, 1), jnp.int32),
            pltpu.VMEM((nb // 2, cols), jnp.int32),
            pltpu.VMEM((nb, steps, cols), bf16),
            pltpu.VMEM((2, steps // HALF_ROWS, cols), f32),
            pltpu.VMEM((mode_cols, nm * patches), bf16),
            pltpu.VMEM((mode_cols, modes), bf16),
            pltpu.VMEM((mode_cols, modes), bf16),
            pltpu.VMEM((nb, nm, patches, cols), bf16),
            pltpu.VMEM((nb, mode_cols, cols), bf16),
            pltpu.VMEM((mode_cols, cols), f32),
            pltpu.VMEM((nb, mode_cols, cols), bf16),
            pltpu.VMEM((nm, mode_cols, cols), bf16),
            pltpu.VMEM((nb, nm, mode_cols, cols), bf16),
            pltpu.VMEM((nm, patches, mode_cols), bf16),
            pltpu.VMEM((patches, steps), f32),
            ]
        + [dma(5)]
        + [dma(nb) for _ in range(10)]
        + [dma(nm) for _ in range(4)]
        + [dma(nb) for _ in range(14)],
        compiler_params=pltpu.CompilerParams(collective_id=0, has_side_effects=True),
    )(velocity[0], radiation_modes, resistance[0], mode_ranks.reshape(1, 1), freq_table.reshape(nb // 2, cols))
    return out[None]


def make_table(freq_table, step_count):
    times = jnp.arange(step_count, dtype=jnp.int32)
    phases = times[:, None] * freq_table[None, :] % step_count
    angles = phases.astype(jnp.float32) * (2.0 * math.pi / step_count)
    norming = 1.0 / math.sqrt(step_count)
    table = jnp.stack([jnp.cos(angles), -jnp.sin(angles)], axis=1) * norming
    return table.astype(jnp.bfloat16)


def add_sources(received):
    return jnp.sum(received, axis=0)


def per_device(velocity, radiation_modes, resistance, mode_ranks, freq_table):
    step_count = velocity.shape[2]
    mode_cols = radiation_modes.shape[1]
    dft_table = make_table(freq_table, step_count)
    spectra = jnp.einsum(
        "wpt,tcf->wpcf", velocity, dft_table, preferred_element_type=jnp.float32
    ).astype(jnp.bfloat16)
    partial_value = jnp.einsum(
        "wpcf,pr->wrcf",
        lax.all_gather(spectra, "mode", axis=1, tiled=True),
        radiation_modes,
        preferred_element_type=jnp.float32,
    )
    coefficients = add_sources(
        lax.all_to_all(
            partial_value[None].astype(jnp.bfloat16),
            "band",
            split_axis=4,
            concat_axis=0,
            tiled=True,
        ).astype(jnp.float32)
    )
    offset = lax.axis_index("mode") * mode_cols
    rank_here = mode_ranks[0]
    kept_mask = (offset + jnp.arange(mode_cols, dtype=jnp.int32) < rank_here).astype(jnp.float32)
    kept_mask = kept_mask[None, :, None, None]
    coefficients = coefficients * kept_mask
    matrix = resistance[0]
    partial_terms = jnp.einsum(
        "ij,wjcf->wicf", matrix, coefficients, precision=lax.Precision.HIGHEST
    )
    forcing = lax.psum_scatter(
        partial_terms.astype(jnp.bfloat16), "mode", scatter_dimension=1, tiled=True
    ).astype(jnp.float32)
    forcing = (2.0 * forcing * kept_mask).astype(jnp.bfloat16)
    collected = lax.all_gather(forcing, "mode", axis=1, tiled=True)
    collected = lax.all_gather(collected, "band", axis=3, tiled=True)
    own_basis = lax.all_to_all(radiation_modes, "mode", split_axis=0, concat_axis=1, tiled=True)
    surface_force = jnp.einsum(
        "pr,wrcf->wpcf", own_basis, collected, preferred_element_type=jnp.float32
    ).astype(jnp.bfloat16)
    history = jnp.einsum(
        "wpcf,tcf->wpt", surface_force, dft_table, preferred_element_type=jnp.float32
    )
    return history.astype(jnp.bfloat16)


def solution(mesh):
    placed = (
        P(None, ("band", "mode"), None),
        P("band", "mode"),
        P("band", None, "mode"),
        P("band"),
        P(),
    )
    nb, nm = mesh.shape["band"], mesh.shape["mode"]

    def body(velocity, radiation_modes, resistance, mode_ranks, freq_table):
        windows, patches, steps = velocity.shape
        mode_cols = radiation_modes.shape[1]
        cols = 2 * (freq_table.shape[0] // nb)
        tiled = (
            windows == 1 and nm == 4 and nb == 8 and cols == 128 and mode_cols % 128 == 0
            and patches % 128 == 0 and steps % 128 == 0 and steps & (steps - 1) == 0
        )
        args = (velocity, radiation_modes, resistance, mode_ranks, freq_table)
        return fused(mesh, *args) if tiled else per_device(*args)

    return jax.shard_map(
        body,
        mesh=mesh,
        in_specs=placed,
        out_specs=P(None, ("band", "mode"), None),
        check_vma=False,
    )
```

```python
import functools
import math

import jax
import jax.numpy as jnp
from jax import lax
from jax.experimental import pallas as pl
from jax.experimental.pallas import tpu as pltpu
from jax.sharding import PartitionSpec as P

MESH = pl.DeviceIdType.MESH
HALF_ROWS = 32


def cosine_of(phase, period):
    wrapped = phase & (period - 1)
    folded = jnp.minimum(wrapped, period - wrapped)
    flip = folded > period // 4
    folded = jnp.where(flip, period // 2 - folded, folded)
    x = folded.astype(jnp.float32) * (2.0 * math.pi / period)
    y = x * x
    value = jnp.full_like(y, 1.0 / math.factorial(16))
    for n in range(14, -1, -2):
        sign = -1.0 if n % 4 else 1.0
        value = value * y + sign / math.factorial(n)
    return jnp.where(flip, -value, value)


def fused_kernel(
    nb, nm, vel_hbm, modes_hbm, res_hbm, rank_hbm, freq_hbm, out_ref,
    vel_ref, modes_ref, res_ref, rank_ref, freq_ref,
    table, trig, modes_t, res_t, spec, part, pend, summed, coef, force, basis, acc,
    in_s, tx, sx_r, sm_r, sf_r, ry_r, rz_r, k_r, ob_r,
    far_r, nu_r, nl_r, cu_r, cl_r, g_r, mf_r,
):
    b = lax.axis_index("band")
    m = lax.axis_index("mode")
    mate = m + 1 - 2 * (m % 2)
    cross = (m + 2) % nm
    here = m // 2
    patches, steps = vel_ref.shape
    cols = table.shape[2]
    mode_cols = modes_ref.shape[1]
    pairs = nb // 2

    def band_at(e):
        bits = [1 << i for i in range(nb.bit_length() - 1)]
        return sum(bit * ((b // bit + e // bit) % 2) for bit in bits)

    near = band_at(1)

    def to_mode(src, dst, send, recv, target):
        return pltpu.make_async_remote_copy(
            src_ref=src, dst_ref=dst, send_sem=tx.at[send], recv_sem=recv,
            device_id={"mode": target}, device_id_type=MESH)

    def to_band(src, dst, send, recv, target):
        return pltpu.make_async_remote_copy(
            src_ref=src, dst_ref=dst, send_sem=tx.at[send], recv_sem=recv,
            device_id={"band": target}, device_id_type=MESH)

    def wait_bytes(ref, sem):
        pltpu.make_async_copy(ref, ref, sem).wait()

    loads = [
        pltpu.make_async_copy(src, dst, in_s.at[i])
        for i, (src, dst) in enumerate((
            (freq_hbm, freq_ref), (vel_hbm, vel_ref), (modes_hbm, modes_ref),
            (res_hbm, res_ref), (rank_hbm, rank_ref)))
    ]
    for load in loads:
        load.start()
    barrier = pltpu.get_barrier_semaphore()
    for off in range(1, nm):
        pl.semaphore_signal(barrier, inc=1, device_id={"mode": (m + off) % nm}, device_id_type=MESH)
    for off in range(1, nb):
        pl.semaphore_signal(barrier, inc=1, device_id={"band": band_at(off)}, device_id_type=MESH)

    blocks = steps // HALF_ROWS
    norming = 1.0 / math.sqrt(steps)

    def build(k):
        half = cols // 2
        lane = lax.broadcasted_iota(jnp.int32, (HALF_ROWS, cols), 1)
        row = jnp.broadcast_to(freq_ref[pl.ds(k // 2, 1), :], (HALF_ROWS, cols))
        freq = jnp.where(lane // half == k % 2, row, pltpu.roll(row, half, 1))
        shift = jnp.where(lane < half, 0, steps // 4)
        rows = lax.broadcasted_iota(jnp.int32, (HALF_ROWS, cols), 0)
        big = lax.broadcasted_iota(jnp.int32, (blocks, cols), 0) * HALF_ROWS
        low = rows * freq + shift
        high = big * freq
        quarter = steps // 4
        cos_low = cosine_of(low, steps) * norming
        sin_low = cosine_of(low - quarter, steps) * norming
        trig[0] = cosine_of(high, steps)
        trig[1] = cosine_of(high - quarter, steps)
        for a in range(blocks):
            row = trig[0, pl.ds(a, 1), :] * cos_low - trig[1, pl.ds(a, 1), :] * sin_low
            table[k, pl.ds(a * HALF_ROWS, HALF_ROWS), :] = row.astype(jnp.bfloat16)

    def project(k):
        spec[k, m] = jnp.dot(
            vel_ref[...], table[k], preferred_element_type=jnp.float32
        ).astype(jnp.bfloat16)

    order = (7, 5, 6, 3, 4, 1, 2, 0)

    def slot(i):
        return band_at(order[i])

    def s_cross(k):
        return to_mode(spec.at[k, m], spec.at[k, m], 0, sx_r.at[k], cross)

    def s_mate(k):
        return to_mode(spec.at[k, m], spec.at[k, m], 0, sm_r.at[0], mate)

    def s_fwd(k):
        return to_mode(spec.at[k, cross], spec.at[k, cross], 0, sf_r.at[k], mate)

    loads[0].wait()
    build(slot(0))
    loads[1].wait()
    project(slot(0))
    pl.semaphore_wait(barrier, nm - 1 + nb - 1)

    for i in range(nb):
        s_cross(slot(i)).start()
        s_mate(slot(i)).start()
        if i < nb - 1:
            build(slot(i + 1))
            project(slot(i + 1))

    def basis_copy(off):
        target = (m + off) % nm
        rows = pl.ds(pl.multiple_of(target * patches, patches), patches)
        return to_mode(modes_ref.at[rows], basis.at[m], 3, ob_r.at[0], target)

    loads[2].wait()
    for off in range(1, nm):
        basis_copy(off).start()
    for half in range(2):
        rows = pl.ds(pl.multiple_of(((here + half) % 2) * 2 * patches, 2 * patches), 2 * patches)
        modes_t[half] = modes_ref[rows, :].T
    wait_bytes(spec.at[pl.ds(0, nb // nm)], sm_r.at[0])

    def partial(k, half):
        chip = pl.ds(pl.multiple_of(((here + half) % 2) * 2, 2), 2)
        return jnp.dot(
            modes_t[half], spec[k, chip].reshape(2 * patches, cols), preferred_element_type=jnp.float32)

    def y_copy(j):
        return to_band(part.at[2 * j + 1], summed.at[j], 1, ry_r.at[j], near)

    def z_copy(j):
        return to_band(part.at[2 * j], summed.at[pairs + j - 1], 1, rz_r.at[j - 1], band_at(2 * j))

    def pass_on(j, value):
        y_copy(j).wait_recv()
        part[2 * j] = (value + summed[j].astype(jnp.float32)).astype(jnp.bfloat16)
        z_copy(j).start()

    for i, e in enumerate(order):
        k = slot(i)
        own = partial(k, 0)
        s_cross(k).wait_recv()
        s_fwd(k).start()
        if e == 3:
            pass_on(3, pend[...])
        s_fwd(k).wait_recv()
        value = own + partial(k, 1)
        if e % 2:
            part[e] = value.astype(jnp.bfloat16)
            y_copy(e // 2).start()
        elif e == 6:
            pend[...] = value
        elif e:
            pass_on(e // 2, value)
        else:
            pend[...] = value
    loads[3].wait()
    res_t[...] = res_ref[...].astype(jnp.bfloat16).T
    loads[4].wait()
    total = pend[...]
    for j in range(pairs - 1, 0, -1):
        z_copy(j).wait_recv()
        total = total + summed[pairs + j - 1].astype(jnp.float32)
    y_copy(0).wait_recv()
    total = total + summed[0].astype(jnp.float32)
    kept = lax.broadcasted_iota(jnp.int32, (mode_cols, cols), 0) + m * mode_cols < rank_ref[...]
    total = jnp.where(kept, total, 0.0)
    coef[m] = total.astype(jnp.bfloat16)

    def k_copy(target):
        return to_mode(coef.at[m], coef.at[m], 2, k_r.at[0], target)

    for target in (cross, (mate + 2) % nm, mate):
        k_copy(target).start()
    wait_bytes(coef.at[pl.ds(0, nm - 1)], k_r.at[0])
    coefs = coef[...].reshape(nm * mode_cols, cols)
    forcing = jnp.dot(res_t[...], coefs, preferred_element_type=jnp.float32)
    forcing = jnp.where(kept, 2.0 * forcing, 0.0)
    force[b, m] = forcing.astype(jnp.bfloat16)

    half = mode_cols // 2
    upper, lower = pl.ds(0, half), pl.ds(half, half)

    def f_far(j):
        piece = force.at[b, m]
        return to_band(piece, piece, 5, far_r.at[j - 1], band_at(2 * j))

    def f_near(j, rows, sem):
        piece = force.at[band_at(2 * j), m, rows]
        return to_band(piece, piece, 4, sem.at[j], near)

    def f_cross(j, rows, sem):
        piece = force.at[band_at(2 * j), m, rows]
        return to_mode(piece, piece, 4, sem.at[j], cross)

    def g_near(j):
        piece = force.at[band_at(2 * j), cross, lower]
        return to_band(piece, piece, 4, g_r.at[j], near)

    def g_cross(j):
        piece = force.at[band_at(2 * j + 1), m, upper]
        return to_mode(piece, piece, 4, g_r.at[j], cross)

    def f_mate(e):
        piece = force.at[band_at(e), m]
        return to_mode(piece, piece, 4, mf_r.at[e], mate)

    def f_fwd(e):
        piece = force.at[band_at(e), cross]
        return to_mode(piece, piece, 4, mf_r.at[e], mate)

    def first(j):
        if j > 0:
            f_far(j).wait_recv()
        f_near(j, upper, nu_r).start()
        f_cross(j, lower, cl_r).start()
        f_near(j, lower, nl_r).start()
        f_cross(j, upper, cu_r).start()
        f_mate(2 * j).start()

    def second(j):
        f_near(j, upper, nu_r).wait_recv()
        g_cross(j).start()
        f_cross(j, lower, cl_r).wait_recv()
        g_near(j).start()
        f_near(j, lower, nl_r).wait_recv()
        f_mate(2 * j + 1).start()
        f_cross(j, upper, cu_r).wait_recv()
        f_fwd(2 * j).start()

    def third(j):
        wait_bytes(force.at[0, 0], g_r.at[j])
        f_fwd(2 * j + 1).start()

    for j in range(1, pairs):
        f_far(j).start()
    first(0)

    wait_bytes(basis.at[pl.ds(0, nm - 1)], ob_r.at[0])
    basis[m] = modes_ref[pl.ds(pl.multiple_of(m * patches, patches), patches), :]

    def surface(k):
        value = jnp.dot(basis[0], force[k, 0], preferred_element_type=jnp.float32)
        for j in range(1, nm):
            value = value + jnp.dot(basis[j], force[k, j], preferred_element_type=jnp.float32)
        return value.astype(jnp.bfloat16)

    def last(e):
        k = band_at(e)
        wait_bytes(force.at[0, pl.ds(0, 2)], mf_r.at[e])
        term = lax.dot_general(
            surface(k), table[k], (((1,), (1,)), ((), ())), preferred_element_type=jnp.float32)
        if e == 0:
            acc[...] = term
        elif e < nb - 1:
            acc[...] += term
        else:
            out_ref[...] = (acc[...] + term).astype(out_ref.dtype)

    second(0)
    first(1)
    first(2)
    last(0)
    third(0)
    first(3)
    last(1)
    second(1)
    last(2)
    second(2)
    third(1)
    last(4)
    second(3)
    last(3)
    third(2)
    last(6)
    third(3)
    last(5)
    last(7)

    wait_bytes(spec.at[pl.ds(0, nb - nb // nm)], tx.at[0])
    wait_bytes(part.at[pl.ds(0, nb - 1)], tx.at[1])
    wait_bytes(coef.at[pl.ds(0, nm - 1)], tx.at[2])
    wait_bytes(basis.at[pl.ds(0, nm - 1)], tx.at[3])
    wait_bytes(force.at[pl.ds(0, nb - 1)], tx.at[4])
    wait_bytes(force.at[0, pl.ds(0, pairs - 1)], tx.at[5])


def fused(mesh, velocity, radiation_modes, resistance, mode_ranks, freq_table):
    nb, nm = mesh.shape["band"], mesh.shape["mode"]
    patches, steps = velocity.shape[1:]
    mode_cols = radiation_modes.shape[1]
    modes = nm * mode_cols
    cols = 2 * (freq_table.shape[0] // nb)
    pairs = nb // 2
    bf16, f32 = jnp.bfloat16, jnp.float32
    sems = (5, 6, nb, 1, nb, pairs, pairs - 1, 1, 1, pairs - 1, pairs, pairs, pairs, pairs, pairs, nb)
    hbm = pl.BlockSpec(memory_space=pltpu.HBM)
    out = pl.pallas_call(
        functools.partial(fused_kernel, nb, nm),
        out_shape=pltpu.VMEM((patches, steps), bf16),
        in_specs=[hbm] * 5,
        out_specs=pl.BlockSpec(memory_space=pltpu.VMEM),
        scratch_shapes=[
            pltpu.VMEM((patches, steps), bf16),
            pltpu.VMEM(radiation_modes.shape, bf16),
            pltpu.VMEM(resistance.shape[1:], f32),
            pltpu.VMEM((1, 1), jnp.int32),
            pltpu.VMEM((pairs, cols), jnp.int32),
            pltpu.VMEM((nb, steps, cols), bf16),
            pltpu.VMEM((2, steps // HALF_ROWS, cols), f32),
            pltpu.VMEM((2, mode_cols, 2 * patches), bf16),
            pltpu.VMEM((mode_cols, modes), bf16),
            pltpu.VMEM((nb, nm, patches, cols), bf16),
            pltpu.VMEM((nb, mode_cols, cols), bf16),
            pltpu.VMEM((mode_cols, cols), f32),
            pltpu.VMEM((nb - 1, mode_cols, cols), bf16),
            pltpu.VMEM((nm, mode_cols, cols), bf16),
            pltpu.VMEM((nb, nm, mode_cols, cols), bf16),
            pltpu.VMEM((nm, patches, mode_cols), bf16),
            pltpu.VMEM((patches, steps), f32),
        ]
        + [pltpu.SemaphoreType.DMA((n,)) for n in sems],
        compiler_params=pltpu.CompilerParams(collective_id=0, has_side_effects=True),
    )(velocity[0], radiation_modes, resistance[0], mode_ranks.reshape(1, 1), freq_table.reshape(pairs, cols))
    return out[None]


def make_table(freq_table, step_count):
    times = jnp.arange(step_count, dtype=jnp.int32)
    phases = times[:, None] * freq_table[None, :] % step_count
    angles = phases.astype(jnp.float32) * (2.0 * math.pi / step_count)
    norming = 1.0 / math.sqrt(step_count)
    table = jnp.stack([jnp.cos(angles), -jnp.sin(angles)], axis=1) * norming
    return table.astype(jnp.bfloat16)


def add_sources(received):
    return jnp.sum(received, axis=0)


def per_device(velocity, radiation_modes, resistance, mode_ranks, freq_table):
    step_count = velocity.shape[2]
    mode_cols = radiation_modes.shape[1]
    dft_table = make_table(freq_table, step_count)
    spectra = jnp.einsum(
        "wpt,tcf->wpcf", velocity, dft_table, preferred_element_type=jnp.float32
    ).astype(jnp.bfloat16)
    partial_value = jnp.einsum(
        "wpcf,pr->wrcf",
        lax.all_gather(spectra, "mode", axis=1, tiled=True),
        radiation_modes,
        preferred_element_type=jnp.float32,
    )
    coefficients = add_sources(
        lax.all_to_all(
            partial_value[None].astype(jnp.bfloat16),
            "band",
            split_axis=4,
            concat_axis=0,
            tiled=True,
        ).astype(jnp.float32)
    )
    offset = lax.axis_index("mode") * mode_cols
    rank_here = mode_ranks[0]
    kept_mask = (offset + jnp.arange(mode_cols, dtype=jnp.int32) < rank_here).astype(jnp.float32)
    kept_mask = kept_mask[None, :, None, None]
    coefficients = coefficients * kept_mask
    matrix = resistance[0]
    partial_terms = jnp.einsum(
        "ij,wjcf->wicf", matrix, coefficients, precision=lax.Precision.HIGHEST
    )
    forcing = lax.psum_scatter(
        partial_terms.astype(jnp.bfloat16), "mode", scatter_dimension=1, tiled=True
    ).astype(jnp.float32)
    forcing = (2.0 * forcing * kept_mask).astype(jnp.bfloat16)
    collected = lax.all_gather(forcing, "mode", axis=1, tiled=True)
    collected = lax.all_gather(collected, "band", axis=3, tiled=True)
    own_basis = lax.all_to_all(radiation_modes, "mode", split_axis=0, concat_axis=1, tiled=True)
    surface_force = jnp.einsum(
        "pr,wrcf->wpcf", own_basis, collected, preferred_element_type=jnp.float32
    ).astype(jnp.bfloat16)
    history = jnp.einsum(
        "wpcf,tcf->wpt", surface_force, dft_table, preferred_element_type=jnp.float32
    )
    return history.astype(jnp.bfloat16)


def solution(mesh):
    placed = (
        P(None, ("band", "mode"), None),
        P("band", "mode"),
        P("band", None, "mode"),
        P("band"),
        P(),
    )
    nb, nm = mesh.shape["band"], mesh.shape["mode"]

    def body(velocity, radiation_modes, resistance, mode_ranks, freq_table):
        windows, patches, steps = velocity.shape
        mode_cols = radiation_modes.shape[1]
        cols = 2 * (freq_table.shape[0] // nb)
        tiled = (
            windows == 1 and nm == 4 and nb == 8 and cols == 128 and mode_cols % 128 == 0
            and patches % 128 == 0 and steps % 128 == 0 and steps & (steps - 1) == 0
        )
        args = (velocity, radiation_modes, resistance, mode_ranks, freq_table)
        return fused(mesh, *args) if tiled else per_device(*args)

    return jax.shard_map(
        body,
        mesh=mesh,
        in_specs=placed,
        out_specs=P(None, ("band", "mode"), None),
        check_vma=False,
    )
```

```python
import functools
import math

import jax
import jax.numpy as jnp
from jax import lax
from jax.experimental import pallas as pl
from jax.experimental.pallas import tpu as pltpu
from jax.sharding import PartitionSpec as P

MESH = pl.DeviceIdType.MESH
HALF_ROWS = 32


def cosine_of(phase, period):
    wrapped = phase & (period - 1)
    folded = jnp.minimum(wrapped, period - wrapped)
    flip = folded > period // 4
    folded = jnp.where(flip, period // 2 - folded, folded)
    x = folded.astype(jnp.float32) * (2.0 * math.pi / period)
    y = x * x
    value = jnp.full_like(y, 1.0 / math.factorial(16))
    for n in range(14, -1, -2):
        sign = -1.0 if n % 4 else 1.0
        value = value * y + sign / math.factorial(n)
    return jnp.where(flip, -value, value)


def fused_kernel(
    nb, nm, vel_hbm, modes_hbm, res_hbm, rank_hbm, freq_hbm, out_ref,
    vel_ref, modes_ref, res_ref, rank_ref, freq_ref,
    table, trig, modes_t, res_t, spec, part, pend, summed, coef, force, basis, acc,
    in_s, tx, sx_r, sm_r, sf_r, ry_r, rz_r, k_r, ob_r,
    far_r, nu_r, nl_r, cu_r, cl_r, g_r, h_r, mf_r,
):
    b = lax.axis_index("band")
    m = lax.axis_index("mode")
    mate = m + 1 - 2 * (m % 2)
    cross = (m + 2) % nm
    here = m // 2
    patches, steps = vel_ref.shape
    cols = table.shape[2]
    mode_cols = modes_ref.shape[1]
    pairs = nb // 2

    def band_at(e):
        bits = [1 << i for i in range(nb.bit_length() - 1)]
        return sum(bit * ((b // bit + e // bit) % 2) for bit in bits)

    near = band_at(1)

    def to_mode(src, dst, send, recv, target):
        return pltpu.make_async_remote_copy(
            src_ref=src, dst_ref=dst, send_sem=tx.at[send], recv_sem=recv,
            device_id={"mode": target}, device_id_type=MESH)

    def to_band(src, dst, send, recv, target):
        return pltpu.make_async_remote_copy(
            src_ref=src, dst_ref=dst, send_sem=tx.at[send], recv_sem=recv,
            device_id={"band": target}, device_id_type=MESH)

    def wait_bytes(ref, sem):
        pltpu.make_async_copy(ref, ref, sem).wait()

    loads = [
        pltpu.make_async_copy(src, dst, in_s.at[i])
        for i, (src, dst) in enumerate((
            (freq_hbm, freq_ref), (vel_hbm, vel_ref), (modes_hbm, modes_ref),
            (res_hbm, res_ref), (rank_hbm, rank_ref)))
    ]
    for load in loads:
        load.start()
    barrier = pltpu.get_barrier_semaphore()
    for off in range(1, nm):
        pl.semaphore_signal(barrier, inc=1, device_id={"mode": (m + off) % nm}, device_id_type=MESH)
    for off in range(1, nb):
        pl.semaphore_signal(barrier, inc=1, device_id={"band": band_at(off)}, device_id_type=MESH)

    blocks = steps // HALF_ROWS
    norming = 1.0 / math.sqrt(steps)

    def build(k):
        half = cols // 2
        lane = lax.broadcasted_iota(jnp.int32, (HALF_ROWS, cols), 1)
        row = jnp.broadcast_to(freq_ref[pl.ds(k // 2, 1), :], (HALF_ROWS, cols))
        freq = jnp.where(lane // half == k % 2, row, pltpu.roll(row, half, 1))
        shift = jnp.where(lane < half, 0, steps // 4)
        rows = lax.broadcasted_iota(jnp.int32, (HALF_ROWS, cols), 0)
        big = lax.broadcasted_iota(jnp.int32, (blocks, cols), 0) * HALF_ROWS
        low = rows * freq + shift
        high = big * freq
        quarter = steps // 4
        cos_low = cosine_of(low, steps) * norming
        sin_low = cosine_of(low - quarter, steps) * norming
        trig[0] = cosine_of(high, steps)
        trig[1] = cosine_of(high - quarter, steps)
        for a in range(blocks):
            row = trig[0, pl.ds(a, 1), :] * cos_low - trig[1, pl.ds(a, 1), :] * sin_low
            table[k, pl.ds(a * HALF_ROWS, HALF_ROWS), :] = row.astype(jnp.bfloat16)

    def project(k):
        spec[k, m] = jnp.dot(
            vel_ref[...], table[k], preferred_element_type=jnp.float32
        ).astype(jnp.bfloat16)

    order = (7, 5, 6, 3, 4, 1, 2, 0)

    def slot(i):
        return band_at(order[i])

    def s_cross(k):
        return to_mode(spec.at[k, m], spec.at[k, m], 0, sx_r.at[k], cross)

    def s_mate(k):
        return to_mode(spec.at[k, m], spec.at[k, m], 0, sm_r.at[0], mate)

    def s_fwd(k):
        return to_mode(spec.at[k, cross], spec.at[k, cross], 0, sf_r.at[k], mate)

    loads[0].wait()
    build(slot(0))
    loads[1].wait()
    project(slot(0))
    pl.semaphore_wait(barrier, nm - 1 + nb - 1)

    for i in range(nb):
        s_cross(slot(i)).start()
        s_mate(slot(i)).start()
        if i < nb - 1:
            build(slot(i + 1))
            project(slot(i + 1))

    def basis_copy(off):
        target = (m + off) % nm
        rows = pl.ds(pl.multiple_of(target * patches, patches), patches)
        return to_mode(modes_ref.at[rows], basis.at[m], 3, ob_r.at[0], target)

    loads[2].wait()
    for off in range(1, nm):
        basis_copy(off).start()
    for half in range(2):
        rows = pl.ds(pl.multiple_of(((here + half) % 2) * 2 * patches, 2 * patches), 2 * patches)
        modes_t[half] = modes_ref[rows, :].T
    wait_bytes(spec.at[pl.ds(0, nb // nm)], sm_r.at[0])

    def partial(k, half):
        chip = pl.ds(pl.multiple_of(((here + half) % 2) * 2, 2), 2)
        return jnp.dot(
            modes_t[half], spec[k, chip].reshape(2 * patches, cols), preferred_element_type=jnp.float32)

    def y_copy(j):
        return to_band(part.at[2 * j + 1], summed.at[j], 1, ry_r.at[j], near)

    def z_copy(j):
        return to_band(part.at[2 * j], summed.at[pairs + j - 1], 1, rz_r.at[j - 1], band_at(2 * j))

    def pass_on(j, value):
        y_copy(j).wait_recv()
        part[2 * j] = (value + summed[j].astype(jnp.float32)).astype(jnp.bfloat16)
        z_copy(j).start()

    for i, e in enumerate(order):
        k = slot(i)
        own = partial(k, 0)
        s_cross(k).wait_recv()
        s_fwd(k).start()
        if e == 3:
            pass_on(3, pend[...])
        s_fwd(k).wait_recv()
        value = own + partial(k, 1)
        if e % 2:
            part[e] = value.astype(jnp.bfloat16)
            y_copy(e // 2).start()
        elif e == 6:
            pend[...] = value
        elif e:
            pass_on(e // 2, value)
        else:
            pend[...] = value
    loads[3].wait()
    res_t[...] = res_ref[...].astype(jnp.bfloat16).T
    loads[4].wait()
    total = pend[...]
    for j in range(pairs - 1, 0, -1):
        z_copy(j).wait_recv()
        total = total + summed[pairs + j - 1].astype(jnp.float32)
    y_copy(0).wait_recv()
    total = total + summed[0].astype(jnp.float32)
    kept = lax.broadcasted_iota(jnp.int32, (mode_cols, cols), 0) + m * mode_cols < rank_ref[...]
    total = jnp.where(kept, total, 0.0)
    coef[m] = total.astype(jnp.bfloat16)

    split = mode_cols * 5 // 8 // 16 * 16
    head, tail = pl.ds(0, split), pl.ds(split, mode_cols - split)

    def k_copy(source, rows, sem, target):
        piece = coef.at[source, rows]
        return to_mode(piece, piece, 2, k_r.at[sem], target)

    k_copy(m, head, 0, cross).start()
    k_copy(m, tail, 1, cross).start()
    k_copy(m, tail, 2, (mate + 2) % nm).start()
    k_copy(m, head, 3, mate).start()
    k_copy(m, tail, 4, mate).start()
    k_copy(cross, head, 0, cross).wait_recv()
    k_copy(cross, head, 5, mate).start()
    for rows, sem in ((tail, 1), (tail, 2), (head, 3), (tail, 4), (head, 5)):
        k_copy(m, rows, sem, mate).wait_recv()
    coefs = coef[...].reshape(nm * mode_cols, cols)
    forcing = jnp.dot(res_t[...], coefs, preferred_element_type=jnp.float32)
    forcing = jnp.where(kept, 2.0 * forcing, 0.0)
    force[b, m] = forcing.astype(jnp.bfloat16)

    half = mode_cols // 2
    upper, lower = pl.ds(0, half), pl.ds(half, half)

    def f_far(j):
        piece = force.at[b, m]
        return to_band(piece, piece, 5, far_r.at[j - 1], band_at(2 * j))

    def f_near(j, rows, sem):
        piece = force.at[band_at(2 * j), m, rows]
        return to_band(piece, piece, 4, sem.at[j], near)

    def f_cross(j, rows, sem):
        piece = force.at[band_at(2 * j), m, rows]
        return to_mode(piece, piece, 4, sem.at[j], cross)

    def g_near(j):
        piece = force.at[band_at(2 * j), cross, lower]
        return to_band(piece, piece, 4, g_r.at[j], near)

    def g_cross(j):
        piece = force.at[band_at(2 * j + 1), m, upper]
        return to_mode(piece, piece, 4, g_r.at[j], cross)

    def f_diag(j):
        piece = force.at[band_at(2 * j), m]
        return pltpu.make_async_remote_copy(
            src_ref=piece, dst_ref=piece, send_sem=tx.at[4], recv_sem=g_r.at[j],
            device_id={"band": near, "mode": cross}, device_id_type=MESH)

    def h_near():
        piece = force.at[near, m]
        return to_band(piece, piece, 4, h_r.at[0], band_at(2))

    def h_cross():
        piece = force.at[b, cross]
        return to_band(piece, piece, 4, h_r.at[1], band_at(2))

    def f_mate(e):
        piece = force.at[band_at(e), m]
        return to_mode(piece, piece, 4, mf_r.at[e], mate)

    def f_fwd(e):
        piece = force.at[band_at(e), cross]
        return to_mode(piece, piece, 4, mf_r.at[e], mate)

    def arrived(j):
        f_far(j).wait_recv()

    def first(j):
        if j != 1:
            f_near(j, upper, nu_r).start()
            f_cross(j, lower, cl_r).start()
            f_near(j, lower, nl_r).start()
            f_cross(j, upper, cu_r).start()
        f_mate(2 * j).start()

    def second(j):
        if j == 1:
            h_near().wait_recv()
            g_cross(j).start()
            f_mate(2 * j + 1).start()
            h_cross().wait_recv()
            g_near(j).start()
            f_fwd(2 * j).start()
            return
        f_near(j, upper, nu_r).wait_recv()
        if j:
            g_cross(j).start()
        f_cross(j, lower, cl_r).wait_recv()
        if j:
            g_near(j).start()

    def settle(j):
        f_near(j, lower, nl_r).wait_recv()
        if j == 0:
            h_near().start()
        f_mate(2 * j + 1).start()
        f_cross(j, upper, cu_r).wait_recv()
        if j == 0:
            h_cross().start()
        f_fwd(2 * j).start()

    def third(j):
        wait_bytes(force.at[0, 0], g_r.at[j])
        f_fwd(2 * j + 1).start()

    first(0)
    f_diag(0).start()
    for j in (1, 2, 3):
        f_far(j).start()

    wait_bytes(basis.at[pl.ds(0, nm - 1)], ob_r.at[0])
    basis[m] = modes_ref[pl.ds(pl.multiple_of(m * patches, patches), patches), :]

    def surface(k):
        value = jnp.dot(basis[0], force[k, 0], preferred_element_type=jnp.float32)
        for j in range(1, nm):
            value = value + jnp.dot(basis[j], force[k, j], preferred_element_type=jnp.float32)
        return value.astype(jnp.bfloat16)

    def last(e, place=1):
        k = band_at(e)
        wait_bytes(force.at[0, pl.ds(0, 2)], mf_r.at[e])
        term = lax.dot_general(
            surface(k), table[k], (((1,), (1,)), ((), ())), preferred_element_type=jnp.float32)
        if place == 0:
            acc[...] = term
        elif place == 1:
            acc[...] += term
        else:
            out_ref[...] = (acc[...] + term).astype(out_ref.dtype)

    second(0)
    settle(0)
    arrived(2)
    first(2)
    arrived(1)
    first(1)
    third(0)
    last(0, 0)
    arrived(3)
    first(3)
    last(1, 1)
    second(2)
    settle(2)
    second(1)
    second(3)
    settle(3)
    third(2)
    last(4, 1)
    last(2, 1)
    third(1)
    last(6, 1)
    third(3)
    last(5, 1)
    last(3, 1)
    last(7, 2)
    wait_bytes(spec.at[pl.ds(0, nb - nb // nm)], tx.at[0])
    wait_bytes(part.at[pl.ds(0, nb - 1)], tx.at[1])
    wait_bytes(coef.at[pl.ds(0, nm - 1)], tx.at[2])
    wait_bytes(basis.at[pl.ds(0, nm - 1)], tx.at[3])
    wait_bytes(force.at[pl.ds(0, nb - 1)], tx.at[4])
    wait_bytes(force.at[0, pl.ds(0, pairs - 1)], tx.at[5])


def fused(mesh, velocity, radiation_modes, resistance, mode_ranks, freq_table):
    nb, nm = mesh.shape["band"], mesh.shape["mode"]
    patches, steps = velocity.shape[1:]
    mode_cols = radiation_modes.shape[1]
    modes = nm * mode_cols
    cols = 2 * (freq_table.shape[0] // nb)
    pairs = nb // 2
    bf16, f32 = jnp.bfloat16, jnp.float32
    sems = (5, 6, nb, 1, nb, pairs, pairs - 1, 6, 1, pairs - 1, pairs, pairs, pairs, pairs, pairs, 2, nb)
    hbm = pl.BlockSpec(memory_space=pltpu.HBM)
    out = pl.pallas_call(
        functools.partial(fused_kernel, nb, nm),
        out_shape=pltpu.VMEM((patches, steps), bf16),
        in_specs=[hbm] * 5,
        out_specs=pl.BlockSpec(memory_space=pltpu.VMEM),
        scratch_shapes=[
            pltpu.VMEM((patches, steps), bf16),
            pltpu.VMEM(radiation_modes.shape, bf16),
            pltpu.VMEM(resistance.shape[1:], f32),
            pltpu.VMEM((1, 1), jnp.int32),
            pltpu.VMEM((pairs, cols), jnp.int32),
            pltpu.VMEM((nb, steps, cols), bf16),
            pltpu.VMEM((2, steps // HALF_ROWS, cols), f32),
            pltpu.VMEM((2, mode_cols, 2 * patches), bf16),
            pltpu.VMEM((mode_cols, modes), bf16),
            pltpu.VMEM((nb, nm, patches, cols), bf16),
            pltpu.VMEM((nb, mode_cols, cols), bf16),
            pltpu.VMEM((mode_cols, cols), f32),
            pltpu.VMEM((nb - 1, mode_cols, cols), bf16),
            pltpu.VMEM((nm, mode_cols, cols), bf16),
            pltpu.VMEM((nb, nm, mode_cols, cols), bf16),
            pltpu.VMEM((nm, patches, mode_cols), bf16),
            pltpu.VMEM((patches, steps), f32),
        ]
        + [pltpu.SemaphoreType.DMA((n,)) for n in sems],
        compiler_params=pltpu.CompilerParams(collective_id=0, has_side_effects=True),
    )(velocity[0], radiation_modes, resistance[0], mode_ranks.reshape(1, 1), freq_table.reshape(pairs, cols))
    return out[None]


def make_table(freq_table, step_count):
    times = jnp.arange(step_count, dtype=jnp.int32)
    phases = times[:, None] * freq_table[None, :] % step_count
    angles = phases.astype(jnp.float32) * (2.0 * math.pi / step_count)
    norming = 1.0 / math.sqrt(step_count)
    table = jnp.stack([jnp.cos(angles), -jnp.sin(angles)], axis=1) * norming
    return table.astype(jnp.bfloat16)


def add_sources(received):
    return jnp.sum(received, axis=0)


def per_device(velocity, radiation_modes, resistance, mode_ranks, freq_table):
    step_count = velocity.shape[2]
    mode_cols = radiation_modes.shape[1]
    dft_table = make_table(freq_table, step_count)
    spectra = jnp.einsum(
        "wpt,tcf->wpcf", velocity, dft_table, preferred_element_type=jnp.float32
    ).astype(jnp.bfloat16)
    partial_value = jnp.einsum(
        "wpcf,pr->wrcf",
        lax.all_gather(spectra, "mode", axis=1, tiled=True),
        radiation_modes,
        preferred_element_type=jnp.float32,
    )
    coefficients = add_sources(
        lax.all_to_all(
            partial_value[None].astype(jnp.bfloat16),
            "band",
            split_axis=4,
            concat_axis=0,
            tiled=True,
        ).astype(jnp.float32)
    )
    offset = lax.axis_index("mode") * mode_cols
    rank_here = mode_ranks[0]
    kept_mask = (offset + jnp.arange(mode_cols, dtype=jnp.int32) < rank_here).astype(jnp.float32)
    kept_mask = kept_mask[None, :, None, None]
    coefficients = coefficients * kept_mask
    matrix = resistance[0]
    partial_terms = jnp.einsum(
        "ij,wjcf->wicf", matrix, coefficients, precision=lax.Precision.HIGHEST
    )
    forcing = lax.psum_scatter(
        partial_terms.astype(jnp.bfloat16), "mode", scatter_dimension=1, tiled=True
    ).astype(jnp.float32)
    forcing = (2.0 * forcing * kept_mask).astype(jnp.bfloat16)
    collected = lax.all_gather(forcing, "mode", axis=1, tiled=True)
    collected = lax.all_gather(collected, "band", axis=3, tiled=True)
    own_basis = lax.all_to_all(radiation_modes, "mode", split_axis=0, concat_axis=1, tiled=True)
    surface_force = jnp.einsum(
        "pr,wrcf->wpcf", own_basis, collected, preferred_element_type=jnp.float32
    ).astype(jnp.bfloat16)
    history = jnp.einsum(
        "wpcf,tcf->wpt", surface_force, dft_table, preferred_element_type=jnp.float32
    )
    return history.astype(jnp.bfloat16)


def solution(mesh):
    placed = (
        P(None, ("band", "mode"), None),
        P("band", "mode"),
        P("band", None, "mode"),
        P("band"),
        P(),
    )
    nb, nm = mesh.shape["band"], mesh.shape["mode"]

    def body(velocity, radiation_modes, resistance, mode_ranks, freq_table):
        windows, patches, steps = velocity.shape
        mode_cols = radiation_modes.shape[1]
        cols = 2 * (freq_table.shape[0] // nb)
        tiled = (
            windows == 1 and nm == 4 and nb == 8 and cols == 128 and mode_cols % 128 == 0
            and patches % 128 == 0 and steps % 128 == 0 and steps & (steps - 1) == 0
        )
        args = (velocity, radiation_modes, resistance, mode_ranks, freq_table)
        return fused(mesh, *args) if tiled else per_device(*args)

    return jax.shard_map(
        body,
        mesh=mesh,
        in_specs=placed,
        out_specs=P(None, ("band", "mode"), None),
        check_vma=False,
    )
```

```python
import functools
import math

import jax
import jax.numpy as jnp
from jax import lax
from jax.experimental import pallas as pl
from jax.experimental.pallas import tpu as pltpu
from jax.sharding import PartitionSpec as P

MESH = pl.DeviceIdType.MESH
HALF_ROWS = 32


def cosine_of(phase, period):
    wrapped = phase & (period - 1)
    folded = jnp.minimum(wrapped, period - wrapped)
    flip = folded > period // 4
    folded = jnp.where(flip, period // 2 - folded, folded)
    x = folded.astype(jnp.float32) * (2.0 * math.pi / period)
    y = x * x
    value = jnp.full_like(y, 1.0 / math.factorial(16))
    for n in range(14, -1, -2):
        sign = -1.0 if n % 4 else 1.0
        value = value * y + sign / math.factorial(n)
    return jnp.where(flip, -value, value)


def fused_kernel(
    nb, nm, vel_hbm, modes_hbm, res_hbm, rank_hbm, freq_hbm, out_ref,
    vel_ref, modes_ref, res_ref, rank_ref, freq_ref,
    table, trig, modes_t, res_t, spec, part, pend, summed, coef, force, basis, acc,
    ready, in_s, tx, sx_r, sm_r, sf_r, ry_r, rz_r, k_r, ob_r,
    far_r, nu_r, nl_r, cu_r, cl_r, g_r, h_r, mf_r,
):
    b = lax.axis_index("band")
    m = lax.axis_index("mode")
    mate = m + 1 - 2 * (m % 2)
    cross = (m + 2) % nm
    here = m // 2
    patches, steps = vel_ref.shape
    cols = table.shape[2]
    mode_cols = modes_ref.shape[1]
    pairs = nb // 2
    inner = (b // 2 + 1) // 2 % 2

    def band_at(e):
        bits = [1 << i for i in range(nb.bit_length() - 1)]
        return sum(bit * ((b // bit + e // bit) % 2) for bit in bits)

    near = band_at(1)

    def to_mode(src, dst, send, recv, target):
        return pltpu.make_async_remote_copy(
            src_ref=src, dst_ref=dst, send_sem=tx.at[send], recv_sem=recv,
            device_id={"mode": target}, device_id_type=MESH)

    def to_band(src, dst, send, recv, target):
        return pltpu.make_async_remote_copy(
            src_ref=src, dst_ref=dst, send_sem=tx.at[send], recv_sem=recv,
            device_id={"band": target}, device_id_type=MESH)

    def wait_bytes(ref, sem):
        pltpu.make_async_copy(ref, ref, sem).wait()

    loads = [
        pltpu.make_async_copy(src, dst, in_s.at[i])
        for i, (src, dst) in enumerate((
            (freq_hbm, freq_ref), (vel_hbm, vel_ref), (modes_hbm, modes_ref),
            (res_hbm, res_ref), (rank_hbm, rank_ref)))
    ]
    for load in loads:
        load.start()
    barrier = pltpu.get_barrier_semaphore()
    for off in range(1, nm):
        pl.semaphore_signal(barrier, inc=1, device_id={"mode": (m + off) % nm}, device_id_type=MESH)
    for off in (1, 2):
        pl.semaphore_signal(barrier, inc=1, device_id={"band": band_at(off)}, device_id_type=MESH)

    @pl.when(inner == 1)
    def _():
        pl.semaphore_signal(barrier, inc=1, device_id={"band": band_at(6)}, device_id_type=MESH)

    blocks = steps // HALF_ROWS
    norming = 1.0 / math.sqrt(steps)

    def build(k):
        half = cols // 2
        lane = lax.broadcasted_iota(jnp.int32, (HALF_ROWS, cols), 1)
        row = jnp.broadcast_to(freq_ref[pl.ds(k // 2, 1), :], (HALF_ROWS, cols))
        freq = jnp.where(lane // half == k % 2, row, pltpu.roll(row, half, 1))
        shift = jnp.where(lane < half, 0, steps // 4)
        rows = lax.broadcasted_iota(jnp.int32, (HALF_ROWS, cols), 0)
        big = lax.broadcasted_iota(jnp.int32, (blocks, cols), 0) * HALF_ROWS
        low = rows * freq + shift
        high = big * freq
        quarter = steps // 4
        cos_low = cosine_of(low, steps) * norming
        sin_low = cosine_of(low - quarter, steps) * norming
        trig[0] = cosine_of(high, steps)
        trig[1] = cosine_of(high - quarter, steps)
        for a in range(blocks):
            row = trig[0, pl.ds(a, 1), :] * cos_low - trig[1, pl.ds(a, 1), :] * sin_low
            table[k, pl.ds(a * HALF_ROWS, HALF_ROWS), :] = row.astype(jnp.bfloat16)

    def project(k):
        spec[k, m] = jnp.dot(
            vel_ref[...], table[k], preferred_element_type=jnp.float32
        ).astype(jnp.bfloat16)

    order = (7, 5, 6, 3, 4, 1, 2, 0)

    def slot(i):
        return band_at(order[i])

    def s_cross(k):
        return to_mode(spec.at[k, m], spec.at[k, m], 0, sx_r.at[k], cross)

    def s_mate(k):
        return to_mode(spec.at[k, m], spec.at[k, m], 0, sm_r.at[0], mate)

    def s_fwd(k):
        return to_mode(spec.at[k, cross], spec.at[k, cross], 0, sf_r.at[k], mate)

    loads[0].wait()
    build(slot(0))
    loads[1].wait()
    project(slot(0))
    pl.semaphore_wait(barrier, nm + 1 + inner)

    @pl.when(inner == 1)
    def _():
        pl.semaphore_signal(ready, inc=1, device_id={"band": band_at(6)}, device_id_type=MESH)

    for i in range(nb):
        s_cross(slot(i)).start()
        s_mate(slot(i)).start()
        if i < nb - 1:
            build(slot(i + 1))
            project(slot(i + 1))

    def basis_copy(off):
        target = (m + off) % nm
        rows = pl.ds(pl.multiple_of(target * patches, patches), patches)
        return to_mode(modes_ref.at[rows], basis.at[m], 3, ob_r.at[0], target)

    loads[2].wait()
    for off in range(1, nm):
        basis_copy(off).start()

    @pl.when(inner == 1)
    def _():
        pl.semaphore_wait(ready, 1)
        pl.semaphore_signal(ready, inc=1, device_id={"band": band_at(2)}, device_id_type=MESH)

    for half in range(2):
        rows = pl.ds(pl.multiple_of(((here + half) % 2) * 2 * patches, 2 * patches), 2 * patches)
        modes_t[half] = modes_ref[rows, :].T
    wait_bytes(spec.at[pl.ds(0, nb // nm)], sm_r.at[0])

    def partial(k, half):
        chip = pl.ds(pl.multiple_of(((here + half) % 2) * 2, 2), 2)
        return jnp.dot(
            modes_t[half], spec[k, chip].reshape(2 * patches, cols), preferred_element_type=jnp.float32)

    def y_copy(j):
        return to_band(part.at[2 * j + 1], summed.at[j], 1, ry_r.at[j], near)

    def z_copy(j):
        return to_band(part.at[2 * j], summed.at[pairs + j - 1], 1, rz_r.at[j - 1], band_at(2 * j))

    def pass_on(j, value):
        y_copy(j).wait_recv()
        part[2 * j] = (value + summed[j].astype(jnp.float32)).astype(jnp.bfloat16)
        z_copy(j).start()

    for i, e in enumerate(order):
        k = slot(i)
        own = partial(k, 0)
        s_cross(k).wait_recv()
        s_fwd(k).start()
        if e == 3:
            @pl.when(inner == 0)
            def _():
                pl.semaphore_wait(ready, 1)

            pass_on(3, pend[...])
        s_fwd(k).wait_recv()
        value = own + partial(k, 1)
        if e % 2:
            part[e] = value.astype(jnp.bfloat16)
            y_copy(e // 2).start()
        elif e == 6:
            pend[...] = value
        elif e:
            pass_on(e // 2, value)
        else:
            pend[...] = value
    loads[3].wait()
    res_t[...] = res_ref[...].astype(jnp.bfloat16).T
    loads[4].wait()
    total = pend[...]
    for j in range(pairs - 1, 0, -1):
        z_copy(j).wait_recv()
        total = total + summed[pairs + j - 1].astype(jnp.float32)
    y_copy(0).wait_recv()
    total = total + summed[0].astype(jnp.float32)
    kept = lax.broadcasted_iota(jnp.int32, (mode_cols, cols), 0) + m * mode_cols < rank_ref[...]
    total = jnp.where(kept, total, 0.0)
    coef[m] = total.astype(jnp.bfloat16)

    split = mode_cols * 5 // 8 // 16 * 16
    head, tail = pl.ds(0, split), pl.ds(split, mode_cols - split)

    def k_copy(source, rows, sem, target):
        piece = coef.at[source, rows]
        return to_mode(piece, piece, 2, k_r.at[sem], target)

    k_copy(m, head, 0, cross).start()
    k_copy(m, tail, 1, cross).start()
    k_copy(m, tail, 2, (mate + 2) % nm).start()
    k_copy(m, head, 3, mate).start()
    k_copy(m, tail, 4, mate).start()
    k_copy(cross, head, 0, cross).wait_recv()
    k_copy(cross, head, 5, mate).start()
    for rows, sem in ((tail, 1), (tail, 2), (head, 3), (tail, 4), (head, 5)):
        k_copy(m, rows, sem, mate).wait_recv()
    coefs = coef[...].reshape(nm * mode_cols, cols)
    forcing = jnp.dot(res_t[...], coefs, preferred_element_type=jnp.float32)
    forcing = jnp.where(kept, 2.0 * forcing, 0.0)
    force[b, m] = forcing.astype(jnp.bfloat16)

    half = mode_cols // 2
    upper, lower = pl.ds(0, half), pl.ds(half, half)

    def f_far(j):
        piece = force.at[b, m]
        return to_band(piece, piece, 5, far_r.at[j - 1], band_at(2 * j))

    def f_near(j, rows, sem):
        piece = force.at[band_at(2 * j), m, rows]
        return to_band(piece, piece, 4, sem.at[j], near)

    def f_cross(j, rows, sem):
        piece = force.at[band_at(2 * j), m, rows]
        return to_mode(piece, piece, 4, sem.at[j], cross)

    def g_near(j):
        piece = force.at[band_at(2 * j), cross, lower]
        return to_band(piece, piece, 4, g_r.at[j], near)

    def g_cross(j):
        piece = force.at[band_at(2 * j + 1), m, upper]
        return to_mode(piece, piece, 4, g_r.at[j], cross)

    def f_diag(j):
        piece = force.at[band_at(2 * j), m]
        return pltpu.make_async_remote_copy(
            src_ref=piece, dst_ref=piece, send_sem=tx.at[4], recv_sem=g_r.at[j],
            device_id={"band": near, "mode": cross}, device_id_type=MESH)

    def h_near():
        piece = force.at[near, m]
        return to_band(piece, piece, 4, h_r.at[0], band_at(2))

    def h_cross():
        piece = force.at[b, cross]
        return to_band(piece, piece, 4, h_r.at[1], band_at(2))

    def f_mate(e):
        piece = force.at[band_at(e), m]
        return to_mode(piece, piece, 4, mf_r.at[e], mate)

    def f_fwd(e):
        piece = force.at[band_at(e), cross]
        return to_mode(piece, piece, 4, mf_r.at[e], mate)

    def arrived(j):
        f_far(j).wait_recv()

    def first(j):
        if j != 1:
            f_near(j, upper, nu_r).start()
            f_cross(j, lower, cl_r).start()
            f_near(j, lower, nl_r).start()
            f_cross(j, upper, cu_r).start()
        f_mate(2 * j).start()

    def second(j):
        if j == 1:
            h_near().wait_recv()
            g_cross(j).start()
            f_mate(2 * j + 1).start()
            h_cross().wait_recv()
            g_near(j).start()
            f_fwd(2 * j).start()
            return
        f_near(j, upper, nu_r).wait_recv()
        if j:
            g_cross(j).start()
        f_cross(j, lower, cl_r).wait_recv()
        if j:
            g_near(j).start()

    def settle(j):
        f_near(j, lower, nl_r).wait_recv()
        if j == 0:
            h_near().start()
        f_mate(2 * j + 1).start()
        f_cross(j, upper, cu_r).wait_recv()
        if j == 0:
            h_cross().start()
        f_fwd(2 * j).start()

    def third(j):
        wait_bytes(force.at[0, 0], g_r.at[j])
        f_fwd(2 * j + 1).start()

    first(0)
    f_diag(0).start()
    for j in (1, 2, 3):
        f_far(j).start()

    wait_bytes(basis.at[pl.ds(0, nm - 1)], ob_r.at[0])
    basis[m] = modes_ref[pl.ds(pl.multiple_of(m * patches, patches), patches), :]

    def surface(k):
        value = jnp.dot(basis[0], force[k, 0], preferred_element_type=jnp.float32)
        for j in range(1, nm):
            value = value + jnp.dot(basis[j], force[k, j], preferred_element_type=jnp.float32)
        return value.astype(jnp.bfloat16)

    def last(e, place=1):
        k = band_at(e)
        wait_bytes(force.at[0, pl.ds(0, 2)], mf_r.at[e])
        term = lax.dot_general(
            surface(k), table[k], (((1,), (1,)), ((), ())), preferred_element_type=jnp.float32)
        if place == 0:
            acc[...] = term
        elif place == 1:
            acc[...] += term
        else:
            out_ref[...] = (acc[...] + term).astype(out_ref.dtype)

    second(0)
    settle(0)
    arrived(2)
    first(2)
    arrived(1)
    first(1)
    third(0)
    last(0, 0)
    arrived(3)
    first(3)
    last(1, 1)
    second(2)
    settle(2)
    second(1)
    second(3)
    settle(3)
    third(2)
    last(4, 1)
    last(2, 1)
    third(1)
    last(6, 1)
    third(3)
    last(5, 1)
    last(3, 1)
    last(7, 2)
    wait_bytes(spec.at[pl.ds(0, nb - nb // nm)], tx.at[0])
    wait_bytes(part.at[pl.ds(0, nb - 1)], tx.at[1])
    wait_bytes(coef.at[pl.ds(0, nm - 1)], tx.at[2])
    wait_bytes(basis.at[pl.ds(0, nm - 1)], tx.at[3])
    wait_bytes(force.at[pl.ds(0, nb - 1)], tx.at[4])
    wait_bytes(force.at[0, pl.ds(0, pairs - 1)], tx.at[5])


def fused(mesh, velocity, radiation_modes, resistance, mode_ranks, freq_table):
    nb, nm = mesh.shape["band"], mesh.shape["mode"]
    patches, steps = velocity.shape[1:]
    mode_cols = radiation_modes.shape[1]
    modes = nm * mode_cols
    cols = 2 * (freq_table.shape[0] // nb)
    pairs = nb // 2
    bf16, f32 = jnp.bfloat16, jnp.float32
    sems = (5, 6, nb, 1, nb, pairs, pairs - 1, 6, 1, pairs - 1, pairs, pairs, pairs, pairs, pairs, 2, nb)
    hbm = pl.BlockSpec(memory_space=pltpu.HBM)
    out = pl.pallas_call(
        functools.partial(fused_kernel, nb, nm),
        out_shape=pltpu.VMEM((patches, steps), bf16),
        in_specs=[hbm] * 5,
        out_specs=pl.BlockSpec(memory_space=pltpu.VMEM),
        scratch_shapes=[
            pltpu.VMEM((patches, steps), bf16),
            pltpu.VMEM(radiation_modes.shape, bf16),
            pltpu.VMEM(resistance.shape[1:], f32),
            pltpu.VMEM((1, 1), jnp.int32),
            pltpu.VMEM((pairs, cols), jnp.int32),
            pltpu.VMEM((nb, steps, cols), bf16),
            pltpu.VMEM((2, steps // HALF_ROWS, cols), f32),
            pltpu.VMEM((2, mode_cols, 2 * patches), bf16),
            pltpu.VMEM((mode_cols, modes), bf16),
            pltpu.VMEM((nb, nm, patches, cols), bf16),
            pltpu.VMEM((nb, mode_cols, cols), bf16),
            pltpu.VMEM((mode_cols, cols), f32),
            pltpu.VMEM((nb - 1, mode_cols, cols), bf16),
            pltpu.VMEM((nm, mode_cols, cols), bf16),
            pltpu.VMEM((nb, nm, mode_cols, cols), bf16),
            pltpu.VMEM((nm, patches, mode_cols), bf16),
            pltpu.VMEM((patches, steps), f32),
        ]
        + [pltpu.SemaphoreType.REGULAR]
        + [pltpu.SemaphoreType.DMA((n,)) for n in sems],
        compiler_params=pltpu.CompilerParams(collective_id=0, has_side_effects=True),
    )(velocity[0], radiation_modes, resistance[0], mode_ranks.reshape(1, 1), freq_table.reshape(pairs, cols))
    return out[None]


def make_table(freq_table, step_count):
    times = jnp.arange(step_count, dtype=jnp.int32)
    phases = times[:, None] * freq_table[None, :] % step_count
    angles = phases.astype(jnp.float32) * (2.0 * math.pi / step_count)
    norming = 1.0 / math.sqrt(step_count)
    table = jnp.stack([jnp.cos(angles), -jnp.sin(angles)], axis=1) * norming
    return table.astype(jnp.bfloat16)


def add_sources(received):
    return jnp.sum(received, axis=0)


def per_device(velocity, radiation_modes, resistance, mode_ranks, freq_table):
    step_count = velocity.shape[2]
    mode_cols = radiation_modes.shape[1]
    dft_table = make_table(freq_table, step_count)
    spectra = jnp.einsum(
        "wpt,tcf->wpcf", velocity, dft_table, preferred_element_type=jnp.float32
    ).astype(jnp.bfloat16)
    partial_value = jnp.einsum(
        "wpcf,pr->wrcf",
        lax.all_gather(spectra, "mode", axis=1, tiled=True),
        radiation_modes,
        preferred_element_type=jnp.float32,
    )
    coefficients = add_sources(
        lax.all_to_all(
            partial_value[None].astype(jnp.bfloat16),
            "band",
            split_axis=4,
            concat_axis=0,
            tiled=True,
        ).astype(jnp.float32)
    )
    offset = lax.axis_index("mode") * mode_cols
    rank_here = mode_ranks[0]
    kept_mask = (offset + jnp.arange(mode_cols, dtype=jnp.int32) < rank_here).astype(jnp.float32)
    kept_mask = kept_mask[None, :, None, None]
    coefficients = coefficients * kept_mask
    matrix = resistance[0]
    partial_terms = jnp.einsum(
        "ij,wjcf->wicf", matrix, coefficients, precision=lax.Precision.HIGHEST
    )
    forcing = lax.psum_scatter(
        partial_terms.astype(jnp.bfloat16), "mode", scatter_dimension=1, tiled=True
    ).astype(jnp.float32)
    forcing = (2.0 * forcing * kept_mask).astype(jnp.bfloat16)
    collected = lax.all_gather(forcing, "mode", axis=1, tiled=True)
    collected = lax.all_gather(collected, "band", axis=3, tiled=True)
    own_basis = lax.all_to_all(radiation_modes, "mode", split_axis=0, concat_axis=1, tiled=True)
    surface_force = jnp.einsum(
        "pr,wrcf->wpcf", own_basis, collected, preferred_element_type=jnp.float32
    ).astype(jnp.bfloat16)
    history = jnp.einsum(
        "wpcf,tcf->wpt", surface_force, dft_table, preferred_element_type=jnp.float32
    )
    return history.astype(jnp.bfloat16)


def solution(mesh):
    placed = (
        P(None, ("band", "mode"), None),
        P("band", "mode"),
        P("band", None, "mode"),
        P("band"),
        P(),
    )
    nb, nm = mesh.shape["band"], mesh.shape["mode"]

    def body(velocity, radiation_modes, resistance, mode_ranks, freq_table):
        windows, patches, steps = velocity.shape
        mode_cols = radiation_modes.shape[1]
        cols = 2 * (freq_table.shape[0] // nb)
        tiled = (
            windows == 1 and nm == 4 and nb == 8 and cols == 128 and mode_cols % 128 == 0
            and patches % 128 == 0 and steps % 128 == 0 and steps & (steps - 1) == 0
        )
        args = (velocity, radiation_modes, resistance, mode_ranks, freq_table)
        return fused(mesh, *args) if tiled else per_device(*args)

    return jax.shard_map(
        body,
        mesh=mesh,
        in_specs=placed,
        out_specs=P(None, ("band", "mode"), None),
        check_vma=False,
    )
```

```python
import functools
import math

import jax
import jax.numpy as jnp
from jax import lax
from jax.experimental import pallas as pl
from jax.experimental.pallas import tpu as pltpu
from jax.sharding import PartitionSpec as P

MESH = pl.DeviceIdType.MESH
HALF_ROWS = 32


def cosine_of(phase, period):
    wrapped = phase & (period - 1)
    folded = jnp.minimum(wrapped, period - wrapped)
    flip = folded > period // 4
    folded = jnp.where(flip, period // 2 - folded, folded)
    x = folded.astype(jnp.float32) * (2.0 * math.pi / period)
    y = x * x
    value = jnp.full_like(y, 1.0 / math.factorial(16))
    for n in range(14, -1, -2):
        sign = -1.0 if n % 4 else 1.0
        value = value * y + sign / math.factorial(n)
    return jnp.where(flip, -value, value)


def fused_kernel(
    nb, nm, vel_hbm, modes_hbm, res_hbm, rank_hbm, freq_hbm, out_ref,
    vel_ref, modes_ref, res_ref, rank_ref, freq_ref,
    table, trig, modes_t, res_t, spec, part, pend, summed, coef, force, basis, acc,
    ready, in_s, tx, sx_r, sm_r, sf_r, ry_r, rz_r, k_r, ob_r,
    far_r, nu_r, nl_r, cu_r, cl_r, g_r, h_r, mf_r,
):
    b = lax.axis_index("band")
    m = lax.axis_index("mode")
    mate = m + 1 - 2 * (m % 2)
    cross = (m + 2) % nm
    here = m // 2
    patches, steps = vel_ref.shape
    cols = table.shape[2]
    mode_cols = modes_ref.shape[1]
    pairs = nb // 2
    inner = (b // 2 + 1) // 2 % 2

    def band_at(e):
        bits = [1 << i for i in range(nb.bit_length() - 1)]
        return sum(bit * ((b // bit + e // bit) % 2) for bit in bits)

    near = band_at(1)

    def to_mode(src, dst, send, recv, target):
        return pltpu.make_async_remote_copy(
            src_ref=src, dst_ref=dst, send_sem=tx.at[send], recv_sem=recv,
            device_id={"mode": target}, device_id_type=MESH)

    def to_band(src, dst, send, recv, target):
        return pltpu.make_async_remote_copy(
            src_ref=src, dst_ref=dst, send_sem=tx.at[send], recv_sem=recv,
            device_id={"band": target}, device_id_type=MESH)

    def wait_bytes(ref, sem):
        pltpu.make_async_copy(ref, ref, sem).wait()

    loads = [
        pltpu.make_async_copy(src, dst, in_s.at[i])
        for i, (src, dst) in enumerate((
            (freq_hbm, freq_ref), (vel_hbm, vel_ref), (modes_hbm, modes_ref),
            (res_hbm, res_ref), (rank_hbm, rank_ref)))
    ]
    for load in loads:
        load.start()
    barrier = pltpu.get_barrier_semaphore()
    for off in range(1, nm):
        pl.semaphore_signal(barrier, inc=1, device_id={"mode": (m + off) % nm}, device_id_type=MESH)
    for off in (1, 2):
        pl.semaphore_signal(barrier, inc=1, device_id={"band": band_at(off)}, device_id_type=MESH)

    @pl.when(inner == 1)
    def _():
        pl.semaphore_signal(barrier, inc=1, device_id={"band": band_at(6)}, device_id_type=MESH)

    blocks = steps // HALF_ROWS
    norming = 1.0 / math.sqrt(steps)

    def build(k):
        half = cols // 2
        lane = lax.broadcasted_iota(jnp.int32, (HALF_ROWS, cols), 1)
        row = jnp.broadcast_to(freq_ref[pl.ds(k // 2, 1), :], (HALF_ROWS, cols))
        freq = jnp.where(lane // half == k % 2, row, pltpu.roll(row, half, 1))
        shift = jnp.where(lane < half, 0, steps // 4)
        rows = lax.broadcasted_iota(jnp.int32, (HALF_ROWS, cols), 0)
        big = lax.broadcasted_iota(jnp.int32, (blocks, cols), 0) * HALF_ROWS
        low = rows * freq + shift
        high = big * freq
        quarter = steps // 4
        cos_low = cosine_of(low, steps) * norming
        sin_low = cosine_of(low - quarter, steps) * norming
        trig[0] = cosine_of(high, steps)
        trig[1] = cosine_of(high - quarter, steps)
        for a in range(blocks):
            row = trig[0, pl.ds(a, 1), :] * cos_low - trig[1, pl.ds(a, 1), :] * sin_low
            table[k, pl.ds(a * HALF_ROWS, HALF_ROWS), :] = row.astype(jnp.bfloat16)

    def project(k):
        spec[k, m] = jnp.dot(
            vel_ref[...], table[k], preferred_element_type=jnp.float32
        ).astype(jnp.bfloat16)

    order = (7, 5, 6, 3, 4, 1, 2, 0)

    def slot(i):
        return band_at(order[i])

    def s_cross(k):
        return to_mode(spec.at[k, m], spec.at[k, m], 0, sx_r.at[k], cross)

    def s_mate(k):
        return to_mode(spec.at[k, m], spec.at[k, m], 0, sm_r.at[0], mate)

    def s_fwd(k):
        return to_mode(spec.at[k, cross], spec.at[k, cross], 0, sf_r.at[k], mate)

    loads[0].wait()
    build(slot(0))
    loads[1].wait()
    project(slot(0))
    pl.semaphore_wait(barrier, nm + 1 + inner)

    @pl.when(inner == 1)
    def _():
        pl.semaphore_signal(ready, inc=1, device_id={"band": band_at(6)}, device_id_type=MESH)

    for i in range(nb):
        s_cross(slot(i)).start()
        s_mate(slot(i)).start()
        if i < nb - 1:
            build(slot(i + 1))
            project(slot(i + 1))

    def basis_copy(off):
        target = (m + off) % nm
        rows = pl.ds(pl.multiple_of(target * patches, patches), patches)
        return to_mode(modes_ref.at[rows], basis.at[m], 3, ob_r.at[0], target)

    loads[2].wait()
    for off in range(1, nm):
        basis_copy(off).start()

    @pl.when(inner == 1)
    def _():
        pl.semaphore_wait(ready, 1)
        pl.semaphore_signal(ready, inc=1, device_id={"band": band_at(2)}, device_id_type=MESH)

    for half in range(2):
        rows = pl.ds(pl.multiple_of(((here + half) % 2) * 2 * patches, 2 * patches), 2 * patches)
        modes_t[half] = modes_ref[rows, :].T
    wait_bytes(spec.at[pl.ds(0, nb // nm)], sm_r.at[0])

    def partial(k, half):
        chip = pl.ds(pl.multiple_of(((here + half) % 2) * 2, 2), 2)
        return jnp.dot(
            modes_t[half], spec[k, chip].reshape(2 * patches, cols), preferred_element_type=jnp.float32)

    def y_copy(j):
        return to_band(part.at[2 * j + 1], summed.at[j], 1, ry_r.at[j], near)

    def z_copy(j):
        return to_band(part.at[2 * j], summed.at[pairs + j - 1], 1, rz_r.at[j - 1], band_at(2 * j))

    def pass_on(j, value):
        y_copy(j).wait_recv()
        part[2 * j] = (value + summed[j].astype(jnp.float32)).astype(jnp.bfloat16)
        z_copy(j).start()

    for i, e in enumerate(order):
        k = slot(i)
        own = partial(k, 0)
        s_cross(k).wait_recv()
        s_fwd(k).start()
        if e == 3:
            @pl.when(inner == 0)
            def _():
                pl.semaphore_wait(ready, 1)

            pass_on(3, pend[...])
        s_fwd(k).wait_recv()
        value = own + partial(k, 1)
        if e % 2:
            part[e] = value.astype(jnp.bfloat16)
            y_copy(e // 2).start()
        elif e == 6:
            pend[...] = value
        elif e:
            pass_on(e // 2, value)
        else:
            pend[...] = value
    loads[3].wait()
    res_t[...] = res_ref[...].astype(jnp.bfloat16).T
    loads[4].wait()
    total = pend[...]
    for j in range(pairs - 1, 0, -1):
        z_copy(j).wait_recv()
        total = total + summed[pairs + j - 1].astype(jnp.float32)
    y_copy(0).wait_recv()
    total = total + summed[0].astype(jnp.float32)
    kept = lax.broadcasted_iota(jnp.int32, (mode_cols, cols), 0) + m * mode_cols < rank_ref[...]
    total = jnp.where(kept, total, 0.0)
    coef[m] = total.astype(jnp.bfloat16)

    split = mode_cols * 5 // 8 // 16 * 16
    head, tail = pl.ds(0, split), pl.ds(split, mode_cols - split)

    def k_copy(source, rows, sem, target):
        piece = coef.at[source, rows]
        return to_mode(piece, piece, 2, k_r.at[sem], target)

    k_copy(m, head, 0, cross).start()
    k_copy(m, tail, 1, cross).start()
    k_copy(m, tail, 2, (mate + 2) % nm).start()
    k_copy(m, head, 3, mate).start()
    k_copy(m, tail, 4, mate).start()
    k_copy(cross, head, 0, cross).wait_recv()
    k_copy(cross, head, 5, mate).start()
    for rows, sem in ((tail, 1), (tail, 2), (head, 3), (tail, 4), (head, 5)):
        k_copy(m, rows, sem, mate).wait_recv()
    coefs = coef[...].reshape(nm * mode_cols, cols)
    forcing = jnp.dot(res_t[...], coefs, preferred_element_type=jnp.float32)
    forcing = jnp.where(kept, 2.0 * forcing, 0.0)
    force[b, m] = forcing.astype(jnp.bfloat16)

    half = mode_cols // 2
    upper, lower = pl.ds(0, half), pl.ds(half, half)

    def f_far(j):
        piece = force.at[b, m]
        return to_band(piece, piece, 5, far_r.at[j - 1], band_at(2 * j))

    def f_near(j, rows, sem):
        piece = force.at[band_at(2 * j), m, rows]
        return to_band(piece, piece, 4, sem.at[j], near)

    def f_cross(j, rows, sem):
        piece = force.at[band_at(2 * j), m, rows]
        return to_mode(piece, piece, 4, sem.at[j], cross)

    def g_near(j):
        piece = force.at[band_at(2 * j), cross, lower]
        return to_band(piece, piece, 4, g_r.at[j], near)

    def g_cross(j):
        piece = force.at[band_at(2 * j + 1), m, upper]
        return to_mode(piece, piece, 4, g_r.at[j], cross)

    def f_diag(j):
        piece = force.at[band_at(2 * j), m]
        return pltpu.make_async_remote_copy(
            src_ref=piece, dst_ref=piece, send_sem=tx.at[4], recv_sem=g_r.at[j],
            device_id={"band": near, "mode": cross}, device_id_type=MESH)

    def h_near():
        piece = force.at[near, m]
        return to_band(piece, piece, 4, h_r.at[0], band_at(2))

    def h_cross():
        piece = force.at[b, cross]
        return to_band(piece, piece, 4, h_r.at[1], band_at(2))

    def f_mate(e):
        piece = force.at[band_at(e), m]
        return to_mode(piece, piece, 4, mf_r.at[e], mate)

    def f_fwd(e):
        piece = force.at[band_at(e), cross]
        return to_mode(piece, piece, 4, mf_r.at[e], mate)

    def arrived(j):
        f_far(j).wait_recv()

    def first(j):
        if j != 1:
            f_near(j, upper, nu_r).start()
            f_cross(j, lower, cl_r).start()
            f_near(j, lower, nl_r).start()
            f_cross(j, upper, cu_r).start()
        f_mate(2 * j).start()

    def second(j):
        if j == 1:
            h_near().wait_recv()
            g_cross(j).start()
            f_mate(2 * j + 1).start()
            h_cross().wait_recv()
            g_near(j).start()
            f_fwd(2 * j).start()
            return
        f_near(j, upper, nu_r).wait_recv()
        if j:
            g_cross(j).start()
        f_cross(j, lower, cl_r).wait_recv()
        if j:
            g_near(j).start()

    def settle(j):
        f_near(j, lower, nl_r).wait_recv()
        if j == 0:
            h_near().start()
        f_mate(2 * j + 1).start()
        f_cross(j, upper, cu_r).wait_recv()
        if j == 0:
            h_cross().start()
        f_fwd(2 * j).start()

    def third(j):
        wait_bytes(force.at[0, 0], g_r.at[j])
        f_fwd(2 * j + 1).start()

    first(0)
    f_diag(0).start()
    f_far(1).start()
    f_far(3 - inner).start()

    @pl.when(inner == 0)
    def _():
        f_far(2).start()


    wait_bytes(basis.at[pl.ds(0, nm - 1)], ob_r.at[0])
    basis[m] = modes_ref[pl.ds(pl.multiple_of(m * patches, patches), patches), :]

    def surface(k):
        value = jnp.dot(basis[0], force[k, 0], preferred_element_type=jnp.float32)
        for j in range(1, nm):
            value = value + jnp.dot(basis[j], force[k, j], preferred_element_type=jnp.float32)
        return value.astype(jnp.bfloat16)

    def last(e, place=1):
        k = band_at(e)
        wait_bytes(force.at[0, pl.ds(0, 2)], mf_r.at[e])
        term = lax.dot_general(
            surface(k), table[k], (((1,), (1,)), ((), ())), preferred_element_type=jnp.float32)
        if place == 0:
            acc[...] = term
        elif place == 1:
            acc[...] += term
        else:
            out_ref[...] = (acc[...] + term).astype(out_ref.dtype)

    second(0)

    @pl.when(inner == 1)
    def _():
        f_far(3).start()

    settle(0)
    arrived(2)
    first(2)
    arrived(1)
    first(1)
    third(0)
    last(0, 0)
    arrived(3)
    first(3)
    last(1, 1)
    second(2)
    settle(2)
    second(1)
    second(3)
    settle(3)
    third(2)
    last(4, 1)
    last(2, 1)
    third(1)
    last(6, 1)
    third(3)
    last(5, 1)
    last(3, 1)
    last(7, 2)

    wait_bytes(spec.at[pl.ds(0, nb - nb // nm)], tx.at[0])
    wait_bytes(part.at[pl.ds(0, nb - 1)], tx.at[1])
    wait_bytes(coef.at[pl.ds(0, nm - 1)], tx.at[2])
    wait_bytes(basis.at[pl.ds(0, nm - 1)], tx.at[3])
    wait_bytes(force.at[pl.ds(0, nb - 1)], tx.at[4])
    wait_bytes(force.at[0, pl.ds(0, pairs - 1)], tx.at[5])


def fused(mesh, velocity, radiation_modes, resistance, mode_ranks, freq_table):
    nb, nm = mesh.shape["band"], mesh.shape["mode"]
    patches, steps = velocity.shape[1:]
    mode_cols = radiation_modes.shape[1]
    modes = nm * mode_cols
    cols = 2 * (freq_table.shape[0] // nb)
    pairs = nb // 2
    bf16, f32 = jnp.bfloat16, jnp.float32
    sems = (5, 6, nb, 1, nb, pairs, pairs - 1, 6, 1, pairs - 1, pairs, pairs, pairs, pairs, pairs, 2, nb)
    hbm = pl.BlockSpec(memory_space=pltpu.HBM)
    out = pl.pallas_call(
        functools.partial(fused_kernel, nb, nm),
        out_shape=pltpu.VMEM((patches, steps), bf16),
        in_specs=[hbm] * 5,
        out_specs=pl.BlockSpec(memory_space=pltpu.VMEM),
        scratch_shapes=[
            pltpu.VMEM((patches, steps), bf16),
            pltpu.VMEM(radiation_modes.shape, bf16),
            pltpu.VMEM(resistance.shape[1:], f32),
            pltpu.VMEM((1, 1), jnp.int32),
            pltpu.VMEM((pairs, cols), jnp.int32),
            pltpu.VMEM((nb, steps, cols), bf16),
            pltpu.VMEM((2, steps // HALF_ROWS, cols), f32),
            pltpu.VMEM((2, mode_cols, 2 * patches), bf16),
            pltpu.VMEM((mode_cols, modes), bf16),
            pltpu.VMEM((nb, nm, patches, cols), bf16),
            pltpu.VMEM((nb, mode_cols, cols), bf16),
            pltpu.VMEM((mode_cols, cols), f32),
            pltpu.VMEM((nb - 1, mode_cols, cols), bf16),
            pltpu.VMEM((nm, mode_cols, cols), bf16),
            pltpu.VMEM((nb, nm, mode_cols, cols), bf16),
            pltpu.VMEM((nm, patches, mode_cols), bf16),
            pltpu.VMEM((patches, steps), f32),
        ]
        + [pltpu.SemaphoreType.REGULAR]
        + [pltpu.SemaphoreType.DMA((n,)) for n in sems],
        compiler_params=pltpu.CompilerParams(collective_id=0, has_side_effects=True),
    )(velocity[0], radiation_modes, resistance[0], mode_ranks.reshape(1, 1), freq_table.reshape(pairs, cols))
    return out[None]


def make_table(freq_table, step_count):
    times = jnp.arange(step_count, dtype=jnp.int32)
    phases = times[:, None] * freq_table[None, :] % step_count
    angles = phases.astype(jnp.float32) * (2.0 * math.pi / step_count)
    norming = 1.0 / math.sqrt(step_count)
    table = jnp.stack([jnp.cos(angles), -jnp.sin(angles)], axis=1) * norming
    return table.astype(jnp.bfloat16)


def add_sources(received):
    return jnp.sum(received, axis=0)


def per_device(velocity, radiation_modes, resistance, mode_ranks, freq_table):
    step_count = velocity.shape[2]
    mode_cols = radiation_modes.shape[1]
    dft_table = make_table(freq_table, step_count)
    spectra = jnp.einsum(
        "wpt,tcf->wpcf", velocity, dft_table, preferred_element_type=jnp.float32
    ).astype(jnp.bfloat16)
    partial_value = jnp.einsum(
        "wpcf,pr->wrcf",
        lax.all_gather(spectra, "mode", axis=1, tiled=True),
        radiation_modes,
        preferred_element_type=jnp.float32,
    )
    coefficients = add_sources(
        lax.all_to_all(
            partial_value[None].astype(jnp.bfloat16),
            "band",
            split_axis=4,
            concat_axis=0,
            tiled=True,
        ).astype(jnp.float32)
    )
    offset = lax.axis_index("mode") * mode_cols
    rank_here = mode_ranks[0]
    kept_mask = (offset + jnp.arange(mode_cols, dtype=jnp.int32) < rank_here).astype(jnp.float32)
    kept_mask = kept_mask[None, :, None, None]
    coefficients = coefficients * kept_mask
    matrix = resistance[0]
    partial_terms = jnp.einsum(
        "ij,wjcf->wicf", matrix, coefficients, precision=lax.Precision.HIGHEST
    )
    forcing = lax.psum_scatter(
        partial_terms.astype(jnp.bfloat16), "mode", scatter_dimension=1, tiled=True
    ).astype(jnp.float32)
    forcing = (2.0 * forcing * kept_mask).astype(jnp.bfloat16)
    collected = lax.all_gather(forcing, "mode", axis=1, tiled=True)
    collected = lax.all_gather(collected, "band", axis=3, tiled=True)
    own_basis = lax.all_to_all(radiation_modes, "mode", split_axis=0, concat_axis=1, tiled=True)
    surface_force = jnp.einsum(
        "pr,wrcf->wpcf", own_basis, collected, preferred_element_type=jnp.float32
    ).astype(jnp.bfloat16)
    history = jnp.einsum(
        "wpcf,tcf->wpt", surface_force, dft_table, preferred_element_type=jnp.float32
    )
    return history.astype(jnp.bfloat16)


def solution(mesh):
    placed = (
        P(None, ("band", "mode"), None),
        P("band", "mode"),
        P("band", None, "mode"),
        P("band"),
        P(),
    )
    nb, nm = mesh.shape["band"], mesh.shape["mode"]

    def body(velocity, radiation_modes, resistance, mode_ranks, freq_table):
        windows, patches, steps = velocity.shape
        mode_cols = radiation_modes.shape[1]
        cols = 2 * (freq_table.shape[0] // nb)
        tiled = (
            windows == 1 and nm == 4 and nb == 8 and cols == 128 and mode_cols % 128 == 0
            and patches % 128 == 0 and steps % 128 == 0 and steps & (steps - 1) == 0
        )
        args = (velocity, radiation_modes, resistance, mode_ranks, freq_table)
        return fused(mesh, *args) if tiled else per_device(*args)

    return jax.shard_map(
        body,
        mesh=mesh,
        in_specs=placed,
        out_specs=P(None, ("band", "mode"), None),
        check_vma=False,
    )
```

```python
import functools
import math

import jax
import jax.numpy as jnp
from jax import lax
from jax.experimental import pallas as pl
from jax.experimental.pallas import tpu as pltpu
from jax.sharding import PartitionSpec as P

MESH = pl.DeviceIdType.MESH
HALF_ROWS = 32


def cosine_of(phase, period):
    wrapped = phase & (period - 1)
    folded = jnp.minimum(wrapped, period - wrapped)
    flip = folded > period // 4
    folded = jnp.where(flip, period // 2 - folded, folded)
    x = folded.astype(jnp.float32) * (2.0 * math.pi / period)
    y = x * x
    value = jnp.full_like(y, 1.0 / math.factorial(16))
    for n in range(14, -1, -2):
        sign = -1.0 if n % 4 else 1.0
        value = value * y + sign / math.factorial(n)
    return jnp.where(flip, -value, value)


def fused_kernel(
    nb, nm, vel_hbm, modes_hbm, res_hbm, rank_hbm, freq_hbm, out_ref,
    vel_ref, modes_ref, res_ref, rank_ref, freq_ref,
    table, trig, modes_t, res_t, spec, part, pend, summed, coef, force, basis, acc,
    ready, in_s, tx, sx_r, sm_r, sf_r, ry_r, rz_r, k_r, ob_r,
    far_r, nu_r, nl_r, cu_r, cl_r, g_r, h_r, mf_r,
):
    b = lax.axis_index("band")
    m = lax.axis_index("mode")
    mate = m + 1 - 2 * (m % 2)
    cross = (m + 2) % nm
    here = m // 2
    patches, steps = vel_ref.shape
    cols = table.shape[2]
    mode_cols = modes_ref.shape[1]
    pairs = nb // 2
    inner = (b // 2 + 1) // 2 % 2

    def band_at(e):
        bits = [1 << i for i in range(nb.bit_length() - 1)]
        return sum(bit * ((b // bit + e // bit) % 2) for bit in bits)

    near = band_at(1)

    def to_mode(src, dst, send, recv, target):
        return pltpu.make_async_remote_copy(
            src_ref=src, dst_ref=dst, send_sem=tx.at[send], recv_sem=recv,
            device_id={"mode": target}, device_id_type=MESH)

    def to_band(src, dst, send, recv, target):
        return pltpu.make_async_remote_copy(
            src_ref=src, dst_ref=dst, send_sem=tx.at[send], recv_sem=recv,
            device_id={"band": target}, device_id_type=MESH)

    def wait_bytes(ref, sem):
        pltpu.make_async_copy(ref, ref, sem).wait()

    loads = [
        pltpu.make_async_copy(src, dst, in_s.at[i])
        for i, (src, dst) in enumerate((
            (freq_hbm, freq_ref), (vel_hbm, vel_ref), (modes_hbm, modes_ref),
            (res_hbm, res_ref), (rank_hbm, rank_ref)))
    ]
    for load in loads:
        load.start()
    barrier = pltpu.get_barrier_semaphore()
    for off in range(1, nm):
        pl.semaphore_signal(barrier, inc=1, device_id={"mode": (m + off) % nm}, device_id_type=MESH)
    for off in (1, 2):
        pl.semaphore_signal(barrier, inc=1, device_id={"band": band_at(off)}, device_id_type=MESH)

    @pl.when(inner == 1)
    def _():
        pl.semaphore_signal(barrier, inc=1, device_id={"band": band_at(6)}, device_id_type=MESH)

    blocks = steps // HALF_ROWS
    norming = 1.0 / math.sqrt(steps)

    def build(k):
        half = cols // 2
        lane = lax.broadcasted_iota(jnp.int32, (HALF_ROWS, cols), 1)
        row = jnp.broadcast_to(freq_ref[pl.ds(k // 2, 1), :], (HALF_ROWS, cols))
        freq = jnp.where(lane // half == k % 2, row, pltpu.roll(row, half, 1))
        shift = jnp.where(lane < half, 0, steps // 4)
        rows = lax.broadcasted_iota(jnp.int32, (HALF_ROWS, cols), 0)
        big = lax.broadcasted_iota(jnp.int32, (blocks, cols), 0) * HALF_ROWS
        low = rows * freq + shift
        high = big * freq
        quarter = steps // 4
        cos_low = cosine_of(low, steps) * norming
        sin_low = cosine_of(low - quarter, steps) * norming
        trig[0] = cosine_of(high, steps)
        trig[1] = cosine_of(high - quarter, steps)
        for a in range(blocks):
            row = trig[0, pl.ds(a, 1), :] * cos_low - trig[1, pl.ds(a, 1), :] * sin_low
            table[k, pl.ds(a * HALF_ROWS, HALF_ROWS), :] = row.astype(jnp.bfloat16)

    def project(k):
        spec[k, m] = jnp.dot(
            vel_ref[...], table[k], preferred_element_type=jnp.float32
        ).astype(jnp.bfloat16)

    order = (7, 5, 6, 3, 4, 1, 2, 0)

    def slot(i):
        return band_at(order[i])

    def s_cross(k):
        return to_mode(spec.at[k, m], spec.at[k, m], 0, sx_r.at[k], cross)

    def s_mate(k):
        return to_mode(spec.at[k, m], spec.at[k, m], 0, sm_r.at[0], mate)

    def s_fwd(k):
        return to_mode(spec.at[k, cross], spec.at[k, cross], 0, sf_r.at[k], mate)

    loads[0].wait()
    build(slot(0))
    loads[1].wait()
    project(slot(0))
    pl.semaphore_wait(barrier, nm + 1 + inner)

    @pl.when(inner == 1)
    def _():
        pl.semaphore_signal(ready, inc=1, device_id={"band": band_at(6)}, device_id_type=MESH)

    for i in range(nb):
        s_cross(slot(i)).start()
        s_mate(slot(i)).start()
        if i < nb - 1:
            build(slot(i + 1))
            project(slot(i + 1))

    def basis_copy(off):
        target = (m + off) % nm
        rows = pl.ds(pl.multiple_of(target * patches, patches), patches)
        return to_mode(modes_ref.at[rows], basis.at[m], 3, ob_r.at[0], target)

    loads[2].wait()
    for off in range(1, nm):
        basis_copy(off).start()

    @pl.when(inner == 1)
    def _():
        pl.semaphore_wait(ready, 1)
        pl.semaphore_signal(ready, inc=1, device_id={"band": band_at(2)}, device_id_type=MESH)

    for half in range(2):
        rows = pl.ds(pl.multiple_of(((here + half) % 2) * 2 * patches, 2 * patches), 2 * patches)
        modes_t[half] = modes_ref[rows, :].T
    wait_bytes(spec.at[pl.ds(0, nb // nm)], sm_r.at[0])

    def partial(k, half):
        chip = pl.ds(pl.multiple_of(((here + half) % 2) * 2, 2), 2)
        return jnp.dot(
            modes_t[half], spec[k, chip].reshape(2 * patches, cols), preferred_element_type=jnp.float32)

    def y_copy(j):
        return to_band(part.at[2 * j + 1], summed.at[j], 1, ry_r.at[j], near)

    def z_copy(j):
        return to_band(part.at[2 * j], summed.at[pairs + j - 1], 1, rz_r.at[j - 1], band_at(2 * j))

    def pass_on(j, value):
        y_copy(j).wait_recv()
        part[2 * j] = (value + summed[j].astype(jnp.float32)).astype(jnp.bfloat16)
        z_copy(j).start()

    for i, e in enumerate(order):
        k = slot(i)
        own = partial(k, 0)
        s_cross(k).wait_recv()
        s_fwd(k).start()
        if e == 3:
            @pl.when(inner == 0)
            def _():
                pl.semaphore_wait(ready, 1)

            pass_on(3, pend[...])
        s_fwd(k).wait_recv()
        value = own + partial(k, 1)
        if e % 2:
            part[e] = value.astype(jnp.bfloat16)
            y_copy(e // 2).start()
        elif e == 6:
            pend[...] = value
        elif e:
            pass_on(e // 2, value)
        else:
            pend[...] = value
    loads[3].wait()
    res_t[...] = res_ref[...].astype(jnp.bfloat16).T
    loads[4].wait()
    total = pend[...]
    for j in range(pairs - 1, 0, -1):
        z_copy(j).wait_recv()
        total = total + summed[pairs + j - 1].astype(jnp.float32)
    y_copy(0).wait_recv()
    total = total + summed[0].astype(jnp.float32)
    kept = lax.broadcasted_iota(jnp.int32, (mode_cols, cols), 0) + m * mode_cols < rank_ref[...]
    total = jnp.where(kept, total, 0.0)
    coef[m] = total.astype(jnp.bfloat16)

    split = mode_cols * 5 // 8 // 16 * 16
    head, tail = pl.ds(0, split), pl.ds(split, mode_cols - split)

    def k_copy(source, rows, sem, target):
        piece = coef.at[source, rows]
        return to_mode(piece, piece, 2, k_r.at[sem], target)

    k_copy(m, head, 0, cross).start()
    k_copy(m, tail, 1, cross).start()
    k_copy(m, tail, 2, (mate + 2) % nm).start()
    k_copy(m, head, 3, mate).start()
    k_copy(m, tail, 4, mate).start()
    k_copy(cross, head, 0, cross).wait_recv()
    k_copy(cross, head, 5, mate).start()
    for rows, sem in ((tail, 1), (tail, 2), (head, 3), (tail, 4), (head, 5)):
        k_copy(m, rows, sem, mate).wait_recv()
    coefs = coef[...].reshape(nm * mode_cols, cols)
    forcing = jnp.dot(res_t[...], coefs, preferred_element_type=jnp.float32)
    forcing = jnp.where(kept, 2.0 * forcing, 0.0)
    force[b, m] = forcing.astype(jnp.bfloat16)

    half = mode_cols // 2
    upper, lower = pl.ds(0, half), pl.ds(half, half)

    def f_far(j):
        piece = force.at[b, m]
        return to_band(piece, piece, 5, far_r.at[j - 1], band_at(2 * j))

    def f_near(j, rows, sem):
        piece = force.at[band_at(2 * j), m, rows]
        return to_band(piece, piece, 4, sem.at[j], near)

    def f_cross(j, rows, sem):
        piece = force.at[band_at(2 * j), m, rows]
        return to_mode(piece, piece, 4, sem.at[j], cross)

    def g_near(j):
        piece = force.at[band_at(2 * j), cross, lower]
        return to_band(piece, piece, 4, g_r.at[j], near)

    def g_cross(j):
        piece = force.at[band_at(2 * j + 1), m, upper]
        return to_mode(piece, piece, 4, g_r.at[j], cross)

    def f_diag(j):
        piece = force.at[band_at(2 * j), m]
        return pltpu.make_async_remote_copy(
            src_ref=piece, dst_ref=piece, send_sem=tx.at[4], recv_sem=g_r.at[j],
            device_id={"band": near, "mode": cross}, device_id_type=MESH)

    def h_near():
        piece = force.at[near, m]
        return to_band(piece, piece, 4, h_r.at[0], band_at(2))

    def h_cross():
        piece = force.at[b, cross]
        return to_band(piece, piece, 4, h_r.at[1], band_at(2))

    def f_mate(e):
        piece = force.at[band_at(e), m]
        return to_mode(piece, piece, 4, mf_r.at[e], mate)

    def f_fwd(e):
        piece = force.at[band_at(e), cross]
        return to_mode(piece, piece, 4, mf_r.at[e], mate)

    def arrived(j):
        f_far(j).wait_recv()

    def first(j):
        if j != 1:
            f_near(j, upper, nu_r).start()
            f_cross(j, lower, cl_r).start()
            f_near(j, lower, nl_r).start()
            f_cross(j, upper, cu_r).start()
        f_mate(2 * j).start()

    def second(j):
        if j == 1:
            h_near().wait_recv()
            g_cross(j).start()
            f_mate(2 * j + 1).start()
            h_cross().wait_recv()
            g_near(j).start()
            f_fwd(2 * j).start()
            return
        f_near(j, upper, nu_r).wait_recv()
        if j:
            g_cross(j).start()
        f_cross(j, lower, cl_r).wait_recv()
        if j:
            g_near(j).start()

    def settle(j):
        f_near(j, lower, nl_r).wait_recv()
        if j == 0:
            h_near().start()
        f_mate(2 * j + 1).start()
        f_cross(j, upper, cu_r).wait_recv()
        if j == 0:
            h_cross().start()
        f_fwd(2 * j).start()

    def third(j):
        wait_bytes(force.at[0, 0], g_r.at[j])
        f_fwd(2 * j + 1).start()

    first(0)
    f_diag(0).start()
    f_far(1).start()
    f_far(3 - inner).start()

    @pl.when(inner == 0)
    def _():
        f_far(2).start()


    @pl.when(inner == 1)
    def _():
        f_far(3).start()

    wait_bytes(basis.at[pl.ds(0, nm - 1)], ob_r.at[0])
    basis[m] = modes_ref[pl.ds(pl.multiple_of(m * patches, patches), patches), :]

    def surface(k):
        value = jnp.dot(basis[0], force[k, 0], preferred_element_type=jnp.float32)
        for j in range(1, nm):
            value = value + jnp.dot(basis[j], force[k, j], preferred_element_type=jnp.float32)
        return value.astype(jnp.bfloat16)

    def last(e, place=1):
        k = band_at(e)
        wait_bytes(force.at[0, pl.ds(0, 2)], mf_r.at[e])
        term = lax.dot_general(
            surface(k), table[k], (((1,), (1,)), ((), ())), preferred_element_type=jnp.float32)
        if place == 0:
            acc[...] = term
        elif place == 1:
            acc[...] += term
        else:
            out_ref[...] = (acc[...] + term).astype(out_ref.dtype)

    second(0)
    settle(0)
    arrived(2)
    first(2)
    arrived(1)
    first(1)
    third(0)
    last(0, 0)
    arrived(3)
    first(3)
    last(1, 1)
    second(2)
    settle(2)
    second(1)
    second(3)
    settle(3)
    third(2)
    last(4, 1)
    last(2, 1)
    third(1)
    last(6, 1)
    third(3)
    last(5, 1)
    last(3, 1)
    last(7, 2)

    wait_bytes(spec.at[pl.ds(0, nb - nb // nm)], tx.at[0])
    wait_bytes(part.at[pl.ds(0, nb - 1)], tx.at[1])
    wait_bytes(coef.at[pl.ds(0, nm - 1)], tx.at[2])
    wait_bytes(basis.at[pl.ds(0, nm - 1)], tx.at[3])
    wait_bytes(force.at[pl.ds(0, nb - 1)], tx.at[4])
    wait_bytes(force.at[0, pl.ds(0, pairs - 1)], tx.at[5])


def fused(mesh, velocity, radiation_modes, resistance, mode_ranks, freq_table):
    nb, nm = mesh.shape["band"], mesh.shape["mode"]
    patches, steps = velocity.shape[1:]
    mode_cols = radiation_modes.shape[1]
    modes = nm * mode_cols
    cols = 2 * (freq_table.shape[0] // nb)
    pairs = nb // 2
    bf16, f32 = jnp.bfloat16, jnp.float32
    sems = (5, 6, nb, 1, nb, pairs, pairs - 1, 6, 1, pairs - 1, pairs, pairs, pairs, pairs, pairs, 2, nb)
    hbm = pl.BlockSpec(memory_space=pltpu.HBM)
    out = pl.pallas_call(
        functools.partial(fused_kernel, nb, nm),
        out_shape=pltpu.VMEM((patches, steps), bf16),
        in_specs=[hbm] * 5,
        out_specs=pl.BlockSpec(memory_space=pltpu.VMEM),
        scratch_shapes=[
            pltpu.VMEM((patches, steps), bf16),
            pltpu.VMEM(radiation_modes.shape, bf16),
            pltpu.VMEM(resistance.shape[1:], f32),
            pltpu.VMEM((1, 1), jnp.int32),
            pltpu.VMEM((pairs, cols), jnp.int32),
            pltpu.VMEM((nb, steps, cols), bf16),
            pltpu.VMEM((2, steps // HALF_ROWS, cols), f32),
            pltpu.VMEM((2, mode_cols, 2 * patches), bf16),
            pltpu.VMEM((mode_cols, modes), bf16),
            pltpu.VMEM((nb, nm, patches, cols), bf16),
            pltpu.VMEM((nb, mode_cols, cols), bf16),
            pltpu.VMEM((mode_cols, cols), f32),
            pltpu.VMEM((nb - 1, mode_cols, cols), bf16),
            pltpu.VMEM((nm, mode_cols, cols), bf16),
            pltpu.VMEM((nb, nm, mode_cols, cols), bf16),
            pltpu.VMEM((nm, patches, mode_cols), bf16),
            pltpu.VMEM((patches, steps), f32),
        ]
        + [pltpu.SemaphoreType.REGULAR]
        + [pltpu.SemaphoreType.DMA((n,)) for n in sems],
        compiler_params=pltpu.CompilerParams(collective_id=0, has_side_effects=True),
    )(velocity[0], radiation_modes, resistance[0], mode_ranks.reshape(1, 1), freq_table.reshape(pairs, cols))
    return out[None]


def make_table(freq_table, step_count):
    times = jnp.arange(step_count, dtype=jnp.int32)
    phases = times[:, None] * freq_table[None, :] % step_count
    angles = phases.astype(jnp.float32) * (2.0 * math.pi / step_count)
    norming = 1.0 / math.sqrt(step_count)
    table = jnp.stack([jnp.cos(angles), -jnp.sin(angles)], axis=1) * norming
    return table.astype(jnp.bfloat16)


def add_sources(received):
    return jnp.sum(received, axis=0)


def per_device(velocity, radiation_modes, resistance, mode_ranks, freq_table):
    step_count = velocity.shape[2]
    mode_cols = radiation_modes.shape[1]
    dft_table = make_table(freq_table, step_count)
    spectra = jnp.einsum(
        "wpt,tcf->wpcf", velocity, dft_table, preferred_element_type=jnp.float32
    ).astype(jnp.bfloat16)
    partial_value = jnp.einsum(
        "wpcf,pr->wrcf",
        lax.all_gather(spectra, "mode", axis=1, tiled=True),
        radiation_modes,
        preferred_element_type=jnp.float32,
    )
    coefficients = add_sources(
        lax.all_to_all(
            partial_value[None].astype(jnp.bfloat16),
            "band",
            split_axis=4,
            concat_axis=0,
            tiled=True,
        ).astype(jnp.float32)
    )
    offset = lax.axis_index("mode") * mode_cols
    rank_here = mode_ranks[0]
    kept_mask = (offset + jnp.arange(mode_cols, dtype=jnp.int32) < rank_here).astype(jnp.float32)
    kept_mask = kept_mask[None, :, None, None]
    coefficients = coefficients * kept_mask
    matrix = resistance[0]
    partial_terms = jnp.einsum(
        "ij,wjcf->wicf", matrix, coefficients, precision=lax.Precision.HIGHEST
    )
    forcing = lax.psum_scatter(
        partial_terms.astype(jnp.bfloat16), "mode", scatter_dimension=1, tiled=True
    ).astype(jnp.float32)
    forcing = (2.0 * forcing * kept_mask).astype(jnp.bfloat16)
    collected = lax.all_gather(forcing, "mode", axis=1, tiled=True)
    collected = lax.all_gather(collected, "band", axis=3, tiled=True)
    own_basis = lax.all_to_all(radiation_modes, "mode", split_axis=0, concat_axis=1, tiled=True)
    surface_force = jnp.einsum(
        "pr,wrcf->wpcf", own_basis, collected, preferred_element_type=jnp.float32
    ).astype(jnp.bfloat16)
    history = jnp.einsum(
        "wpcf,tcf->wpt", surface_force, dft_table, preferred_element_type=jnp.float32
    )
    return history.astype(jnp.bfloat16)


def solution(mesh):
    placed = (
        P(None, ("band", "mode"), None),
        P("band", "mode"),
        P("band", None, "mode"),
        P("band"),
        P(),
    )
    nb, nm = mesh.shape["band"], mesh.shape["mode"]

    def body(velocity, radiation_modes, resistance, mode_ranks, freq_table):
        windows, patches, steps = velocity.shape
        mode_cols = radiation_modes.shape[1]
        cols = 2 * (freq_table.shape[0] // nb)
        tiled = (
            windows == 1 and nm == 4 and nb == 8 and cols == 128 and mode_cols % 128 == 0
            and patches % 128 == 0 and steps % 128 == 0 and steps & (steps - 1) == 0
        )
        args = (velocity, radiation_modes, resistance, mode_ranks, freq_table)
        return fused(mesh, *args) if tiled else per_device(*args)

    return jax.shard_map(
        body,
        mesh=mesh,
        in_specs=placed,
        out_specs=P(None, ("band", "mode"), None),
        check_vma=False,
    )
```

```python
import functools
import math

import jax
import jax.numpy as jnp
from jax import lax
from jax.experimental import pallas as pl
from jax.experimental.pallas import tpu as pltpu
from jax.sharding import PartitionSpec as P

MESH = pl.DeviceIdType.MESH
HALF_ROWS = 32


def cosine_of(phase, period):
    wrapped = phase & (period - 1)
    folded = jnp.minimum(wrapped, period - wrapped)
    flip = folded > period // 4
    folded = jnp.where(flip, period // 2 - folded, folded)
    x = folded.astype(jnp.float32) * (2.0 * math.pi / period)
    y = x * x
    value = jnp.full_like(y, 1.0 / math.factorial(16))
    for n in range(14, -1, -2):
        sign = -1.0 if n % 4 else 1.0
        value = value * y + sign / math.factorial(n)
    return jnp.where(flip, -value, value)


def fused_kernel(
    nb, nm, vel_hbm, modes_hbm, res_hbm, rank_hbm, freq_hbm, out_ref,
    vel_ref, modes_ref, res_ref, rank_ref, freq_ref,
    table, trig, modes_t, res_t, spec, part, pend, summed, coef, force, basis, acc,
    ready, in_s, tx, sx_r, sm_r, sf_r, ry_r, rz_r, k_r, ob_r,
    far_r, nu_r, nl_r, cu_r, cl_r, g_r, h_r, mf_r,
):
    b = lax.axis_index("band")
    m = lax.axis_index("mode")
    mate = m + 1 - 2 * (m % 2)
    cross = (m + 2) % nm
    here = m // 2
    patches, steps = vel_ref.shape
    cols = table.shape[2]
    mode_cols = modes_ref.shape[1]
    pairs = nb // 2
    inner = (b // 2 + 1) // 2 % 2

    def band_at(e):
        bits = [1 << i for i in range(nb.bit_length() - 1)]
        return sum(bit * ((b // bit + e // bit) % 2) for bit in bits)

    near = band_at(1)

    def to_mode(src, dst, send, recv, target):
        return pltpu.make_async_remote_copy(
            src_ref=src, dst_ref=dst, send_sem=tx.at[send], recv_sem=recv,
            device_id={"mode": target}, device_id_type=MESH)

    def to_band(src, dst, send, recv, target):
        return pltpu.make_async_remote_copy(
            src_ref=src, dst_ref=dst, send_sem=tx.at[send], recv_sem=recv,
            device_id={"band": target}, device_id_type=MESH)

    def wait_bytes(ref, sem):
        pltpu.make_async_copy(ref, ref, sem).wait()

    loads = [
        pltpu.make_async_copy(src, dst, in_s.at[i])
        for i, (src, dst) in enumerate((
            (freq_hbm, freq_ref), (vel_hbm, vel_ref), (modes_hbm, modes_ref),
            (res_hbm, res_ref), (rank_hbm, rank_ref)))
    ]
    for load in loads:
        load.start()
    barrier = pltpu.get_barrier_semaphore()
    for off in range(1, nm):
        pl.semaphore_signal(barrier, inc=1, device_id={"mode": (m + off) % nm}, device_id_type=MESH)
    for off in (1, 2):
        pl.semaphore_signal(barrier, inc=1, device_id={"band": band_at(off)}, device_id_type=MESH)

    @pl.when(inner == 1)
    def _():
        pl.semaphore_signal(barrier, inc=1, device_id={"band": band_at(6)}, device_id_type=MESH)

    blocks = steps // HALF_ROWS
    norming = 1.0 / math.sqrt(steps)

    def build(k):
        half = cols // 2
        lane = lax.broadcasted_iota(jnp.int32, (HALF_ROWS, cols), 1)
        row = jnp.broadcast_to(freq_ref[pl.ds(k // 2, 1), :], (HALF_ROWS, cols))
        freq = jnp.where(lane // half == k % 2, row, pltpu.roll(row, half, 1))
        shift = jnp.where(lane < half, 0, steps // 4)
        rows = lax.broadcasted_iota(jnp.int32, (HALF_ROWS, cols), 0)
        big = lax.broadcasted_iota(jnp.int32, (blocks, cols), 0) * HALF_ROWS
        low = rows * freq + shift
        high = big * freq
        quarter = steps // 4
        cos_low = cosine_of(low, steps) * norming
        sin_low = cosine_of(low - quarter, steps) * norming
        trig[0] = cosine_of(high, steps)
        trig[1] = cosine_of(high - quarter, steps)
        for a in range(blocks):
            row = trig[0, pl.ds(a, 1), :] * cos_low - trig[1, pl.ds(a, 1), :] * sin_low
            table[k, pl.ds(a * HALF_ROWS, HALF_ROWS), :] = row.astype(jnp.bfloat16)

    def project(k):
        spec[k, m] = jnp.dot(
            vel_ref[...], table[k], preferred_element_type=jnp.float32
        ).astype(jnp.bfloat16)

    order = (7, 5, 6, 3, 4, 1, 2, 0)

    def slot(i):
        return band_at(order[i])

    def s_cross(k):
        return to_mode(spec.at[k, m], spec.at[k, m], 0, sx_r.at[k], cross)

    def s_mate(k):
        return to_mode(spec.at[k, m], spec.at[k, m], 0, sm_r.at[0], mate)

    def s_fwd(k):
        return to_mode(spec.at[k, cross], spec.at[k, cross], 0, sf_r.at[k], mate)

    loads[0].wait()
    build(slot(0))
    loads[1].wait()
    project(slot(0))
    pl.semaphore_wait(barrier, nm + 1 + inner)

    @pl.when(inner == 1)
    def _():
        pl.semaphore_signal(ready, inc=1, device_id={"band": band_at(6)}, device_id_type=MESH)

    for i in range(nb):
        s_cross(slot(i)).start()
        s_mate(slot(i)).start()
        if i < nb - 1:
            build(slot(i + 1))
            project(slot(i + 1))

    def basis_copy(off):
        target = (m + off) % nm
        rows = pl.ds(pl.multiple_of(target * patches, patches), patches)
        return to_mode(modes_ref.at[rows], basis.at[m], 3, ob_r.at[0], target)

    loads[2].wait()
    for off in range(1, nm):
        basis_copy(off).start()

    @pl.when(inner == 1)
    def _():
        pl.semaphore_wait(ready, 1)
        pl.semaphore_signal(ready, inc=1, device_id={"band": band_at(2)}, device_id_type=MESH)

    for half in range(2):
        rows = pl.ds(pl.multiple_of(((here + half) % 2) * 2 * patches, 2 * patches), 2 * patches)
        modes_t[half] = modes_ref[rows, :].T
    wait_bytes(spec.at[pl.ds(0, nb // nm)], sm_r.at[0])

    def partial(k, half):
        chip = pl.ds(pl.multiple_of(((here + half) % 2) * 2, 2), 2)
        return jnp.dot(
            modes_t[half], spec[k, chip].reshape(2 * patches, cols), preferred_element_type=jnp.float32)

    def y_copy(j):
        return to_band(part.at[2 * j + 1], summed.at[j], 1, ry_r.at[j], near)

    def z_copy(j):
        return to_band(part.at[2 * j], summed.at[pairs + j - 1], 1, rz_r.at[j - 1], band_at(2 * j))

    def pass_on(j, value):
        y_copy(j).wait_recv()
        part[2 * j] = (value + summed[j].astype(jnp.float32)).astype(jnp.bfloat16)
        z_copy(j).start()

    for i, e in enumerate(order):
        k = slot(i)
        own = partial(k, 0)
        s_cross(k).wait_recv()
        s_fwd(k).start()
        if e == 3:
            @pl.when(inner == 0)
            def _():
                pl.semaphore_wait(ready, 1)

            pass_on(3, pend[...])
        s_fwd(k).wait_recv()
        value = own + partial(k, 1)
        if e % 2:
            part[e] = value.astype(jnp.bfloat16)
            y_copy(e // 2).start()
        elif e == 6:
            pend[...] = value
        elif e:
            pass_on(e // 2, value)
        else:
            pend[...] = value
    loads[3].wait()
    res_t[...] = res_ref[...].astype(jnp.bfloat16).T
    loads[4].wait()
    total = pend[...]
    for j in range(pairs - 1, 0, -1):
        z_copy(j).wait_recv()
        total = total + summed[pairs + j - 1].astype(jnp.float32)
    y_copy(0).wait_recv()
    total = total + summed[0].astype(jnp.float32)
    kept = lax.broadcasted_iota(jnp.int32, (mode_cols, cols), 0) + m * mode_cols < rank_ref[...]
    total = jnp.where(kept, total, 0.0)
    coef[m] = total.astype(jnp.bfloat16)

    split = mode_cols * 5 // 8 // 16 * 16
    head, tail = pl.ds(0, split), pl.ds(split, mode_cols - split)

    def k_copy(source, rows, sem, target):
        piece = coef.at[source, rows]
        return to_mode(piece, piece, 2, k_r.at[sem], target)

    def product(half):
        chip = ((here + half) % 2) * 2
        part_t = res_t[:, pl.ds(pl.multiple_of(chip * mode_cols, 2 * mode_cols), 2 * mode_cols)]
        rows = coef[pl.ds(chip, 2)].reshape(2 * mode_cols, cols)
        return jnp.dot(part_t, rows, preferred_element_type=jnp.float32)

    k_copy(m, head, 0, cross).start()
    k_copy(m, tail, 1, cross).start()
    k_copy(m, tail, 1, (mate + 2) % nm).start()
    k_copy(m, pl.ds(0, mode_cols), 2, mate).start()
    k_copy(cross, head, 0, cross).wait_recv()
    k_copy(cross, head, 3, mate).start()
    k_copy(m, pl.ds(0, mode_cols), 2, mate).wait_recv()
    forcing = product(0)
    wait_bytes(coef.at[0, pl.ds(0, 2 * (mode_cols - split))], k_r.at[1])
    k_copy(m, head, 3, mate).wait_recv()
    forcing = forcing + product(1)
    forcing = jnp.where(kept, 2.0 * forcing, 0.0)
    force[b, m] = forcing.astype(jnp.bfloat16)

    half = mode_cols // 2
    upper, lower = pl.ds(0, half), pl.ds(half, half)

    def f_far(j):
        piece = force.at[b, m]
        return to_band(piece, piece, 5, far_r.at[j - 1], band_at(2 * j))

    def f_near(j, rows, sem):
        piece = force.at[band_at(2 * j), m, rows]
        return to_band(piece, piece, 4, sem.at[j], near)

    def f_cross(j, rows, sem):
        piece = force.at[band_at(2 * j), m, rows]
        return to_mode(piece, piece, 4, sem.at[j], cross)

    def g_near(j):
        piece = force.at[band_at(2 * j), cross, lower]
        return to_band(piece, piece, 4, g_r.at[j], near)

    def g_cross(j):
        piece = force.at[band_at(2 * j + 1), m, upper]
        return to_mode(piece, piece, 4, g_r.at[j], cross)

    def f_diag(j):
        piece = force.at[band_at(2 * j), m]
        return pltpu.make_async_remote_copy(
            src_ref=piece, dst_ref=piece, send_sem=tx.at[4], recv_sem=g_r.at[j],
            device_id={"band": near, "mode": cross}, device_id_type=MESH)

    def h_near():
        piece = force.at[near, m]
        return to_band(piece, piece, 4, h_r.at[0], band_at(2))

    def h_cross():
        piece = force.at[b, cross]
        return to_band(piece, piece, 4, h_r.at[1], band_at(2))

    def f_mate(e):
        piece = force.at[band_at(e), m]
        return to_mode(piece, piece, 4, mf_r.at[e], mate)

    def f_fwd(e):
        piece = force.at[band_at(e), cross]
        return to_mode(piece, piece, 4, mf_r.at[e], mate)

    def arrived(j):
        f_far(j).wait_recv()

    def first(j):
        if j != 1:
            f_near(j, upper, nu_r).start()
            f_cross(j, lower, cl_r).start()
            f_near(j, lower, nl_r).start()
            f_cross(j, upper, cu_r).start()
        f_mate(2 * j).start()

    def second(j):
        if j == 1:
            h_near().wait_recv()
            g_cross(j).start()
            f_mate(2 * j + 1).start()
            h_cross().wait_recv()
            g_near(j).start()
            f_fwd(2 * j).start()
            return
        f_near(j, upper, nu_r).wait_recv()
        if j:
            g_cross(j).start()
        f_cross(j, lower, cl_r).wait_recv()
        if j:
            g_near(j).start()

    def settle(j):
        f_near(j, lower, nl_r).wait_recv()
        if j == 0:
            h_near().start()
        f_mate(2 * j + 1).start()
        f_cross(j, upper, cu_r).wait_recv()
        if j == 0:
            h_cross().start()
        f_fwd(2 * j).start()

    def third(j):
        wait_bytes(force.at[0, 0], g_r.at[j])
        f_fwd(2 * j + 1).start()

    first(0)
    f_diag(0).start()
    f_far(1).start()
    f_far(3 - inner).start()

    @pl.when(inner == 0)
    def _():
        f_far(2).start()


    wait_bytes(basis.at[pl.ds(0, nm - 1)], ob_r.at[0])
    basis[m] = modes_ref[pl.ds(pl.multiple_of(m * patches, patches), patches), :]

    def surface(k):
        value = jnp.dot(basis[0], force[k, 0], preferred_element_type=jnp.float32)
        for j in range(1, nm):
            value = value + jnp.dot(basis[j], force[k, j], preferred_element_type=jnp.float32)
        return value.astype(jnp.bfloat16)

    def last(e, place=1):
        k = band_at(e)
        wait_bytes(force.at[0, pl.ds(0, 2)], mf_r.at[e])
        term = lax.dot_general(
            surface(k), table[k], (((1,), (1,)), ((), ())), preferred_element_type=jnp.float32)
        if place == 0:
            acc[...] = term
        elif place == 1:
            acc[...] += term
        else:
            out_ref[...] = (acc[...] + term).astype(out_ref.dtype)

    second(0)

    @pl.when(inner == 1)
    def _():
        f_far(3).start()

    settle(0)
    arrived(2)
    first(2)
    arrived(1)
    first(1)
    third(0)
    last(0, 0)
    arrived(3)
    first(3)
    last(1, 1)
    second(2)
    settle(2)
    second(1)
    second(3)
    settle(3)
    third(2)
    last(4, 1)
    last(2, 1)
    third(1)
    last(6, 1)
    third(3)
    last(5, 1)
    last(3, 1)
    last(7, 2)

    wait_bytes(spec.at[pl.ds(0, nb - nb // nm)], tx.at[0])
    wait_bytes(part.at[pl.ds(0, nb - 1)], tx.at[1])
    wait_bytes(coef.at[pl.ds(0, nm - 1)], tx.at[2])
    wait_bytes(basis.at[pl.ds(0, nm - 1)], tx.at[3])
    wait_bytes(force.at[pl.ds(0, nb - 1)], tx.at[4])
    wait_bytes(force.at[0, pl.ds(0, pairs - 1)], tx.at[5])


def fused(mesh, velocity, radiation_modes, resistance, mode_ranks, freq_table):
    nb, nm = mesh.shape["band"], mesh.shape["mode"]
    patches, steps = velocity.shape[1:]
    mode_cols = radiation_modes.shape[1]
    modes = nm * mode_cols
    cols = 2 * (freq_table.shape[0] // nb)
    pairs = nb // 2
    bf16, f32 = jnp.bfloat16, jnp.float32
    sems = (5, 6, nb, 1, nb, pairs, pairs - 1, 4, 1, pairs - 1, pairs, pairs, pairs, pairs, pairs, 2, nb)
    hbm = pl.BlockSpec(memory_space=pltpu.HBM)
    out = pl.pallas_call(
        functools.partial(fused_kernel, nb, nm),
        out_shape=pltpu.VMEM((patches, steps), bf16),
        in_specs=[hbm] * 5,
        out_specs=pl.BlockSpec(memory_space=pltpu.VMEM),
        scratch_shapes=[
            pltpu.VMEM((patches, steps), bf16),
            pltpu.VMEM(radiation_modes.shape, bf16),
            pltpu.VMEM(resistance.shape[1:], f32),
            pltpu.VMEM((1, 1), jnp.int32),
            pltpu.VMEM((pairs, cols), jnp.int32),
            pltpu.VMEM((nb, steps, cols), bf16),
            pltpu.VMEM((2, steps // HALF_ROWS, cols), f32),
            pltpu.VMEM((2, mode_cols, 2 * patches), bf16),
            pltpu.VMEM((mode_cols, modes), bf16),
            pltpu.VMEM((nb, nm, patches, cols), bf16),
            pltpu.VMEM((nb, mode_cols, cols), bf16),
            pltpu.VMEM((mode_cols, cols), f32),
            pltpu.VMEM((nb - 1, mode_cols, cols), bf16),
            pltpu.VMEM((nm, mode_cols, cols), bf16),
            pltpu.VMEM((nb, nm, mode_cols, cols), bf16),
            pltpu.VMEM((nm, patches, mode_cols), bf16),
            pltpu.VMEM((patches, steps), f32),
        ]
        + [pltpu.SemaphoreType.REGULAR]
        + [pltpu.SemaphoreType.DMA((n,)) for n in sems],
        compiler_params=pltpu.CompilerParams(collective_id=0, has_side_effects=True),
    )(velocity[0], radiation_modes, resistance[0], mode_ranks.reshape(1, 1), freq_table.reshape(pairs, cols))
    return out[None]


def make_table(freq_table, step_count):
    times = jnp.arange(step_count, dtype=jnp.int32)
    phases = times[:, None] * freq_table[None, :] % step_count
    angles = phases.astype(jnp.float32) * (2.0 * math.pi / step_count)
    norming = 1.0 / math.sqrt(step_count)
    table = jnp.stack([jnp.cos(angles), -jnp.sin(angles)], axis=1) * norming
    return table.astype(jnp.bfloat16)


def add_sources(received):
    return jnp.sum(received, axis=0)


def per_device(velocity, radiation_modes, resistance, mode_ranks, freq_table):
    step_count = velocity.shape[2]
    mode_cols = radiation_modes.shape[1]
    dft_table = make_table(freq_table, step_count)
    spectra = jnp.einsum(
        "wpt,tcf->wpcf", velocity, dft_table, preferred_element_type=jnp.float32
    ).astype(jnp.bfloat16)
    partial_value = jnp.einsum(
        "wpcf,pr->wrcf",
        lax.all_gather(spectra, "mode", axis=1, tiled=True),
        radiation_modes,
        preferred_element_type=jnp.float32,
    )
    coefficients = add_sources(
        lax.all_to_all(
            partial_value[None].astype(jnp.bfloat16),
            "band",
            split_axis=4,
            concat_axis=0,
            tiled=True,
        ).astype(jnp.float32)
    )
    offset = lax.axis_index("mode") * mode_cols
    rank_here = mode_ranks[0]
    kept_mask = (offset + jnp.arange(mode_cols, dtype=jnp.int32) < rank_here).astype(jnp.float32)
    kept_mask = kept_mask[None, :, None, None]
    coefficients = coefficients * kept_mask
    matrix = resistance[0]
    partial_terms = jnp.einsum(
        "ij,wjcf->wicf", matrix, coefficients, precision=lax.Precision.HIGHEST
    )
    forcing = lax.psum_scatter(
        partial_terms.astype(jnp.bfloat16), "mode", scatter_dimension=1, tiled=True
    ).astype(jnp.float32)
    forcing = (2.0 * forcing * kept_mask).astype(jnp.bfloat16)
    collected = lax.all_gather(forcing, "mode", axis=1, tiled=True)
    collected = lax.all_gather(collected, "band", axis=3, tiled=True)
    own_basis = lax.all_to_all(radiation_modes, "mode", split_axis=0, concat_axis=1, tiled=True)
    surface_force = jnp.einsum(
        "pr,wrcf->wpcf", own_basis, collected, preferred_element_type=jnp.float32
    ).astype(jnp.bfloat16)
    history = jnp.einsum(
        "wpcf,tcf->wpt", surface_force, dft_table, preferred_element_type=jnp.float32
    )
    return history.astype(jnp.bfloat16)


def solution(mesh):
    placed = (
        P(None, ("band", "mode"), None),
        P("band", "mode"),
        P("band", None, "mode"),
        P("band"),
        P(),
    )
    nb, nm = mesh.shape["band"], mesh.shape["mode"]

    def body(velocity, radiation_modes, resistance, mode_ranks, freq_table):
        windows, patches, steps = velocity.shape
        mode_cols = radiation_modes.shape[1]
        cols = 2 * (freq_table.shape[0] // nb)
        tiled = (
            windows == 1 and nm == 4 and nb == 8 and cols == 128 and mode_cols % 128 == 0
            and patches % 128 == 0 and steps % 128 == 0 and steps & (steps - 1) == 0
        )
        args = (velocity, radiation_modes, resistance, mode_ranks, freq_table)
        return fused(mesh, *args) if tiled else per_device(*args)

    return jax.shard_map(
        body,
        mesh=mesh,
        in_specs=placed,
        out_specs=P(None, ("band", "mode"), None),
        check_vma=False,
    )
```

```python
import functools
import math

import jax
import jax.numpy as jnp
from jax import lax
from jax.experimental import pallas as pl
from jax.experimental.pallas import tpu as pltpu
from jax.sharding import PartitionSpec as P

MESH = pl.DeviceIdType.MESH
HALF_ROWS = 32


def cosine_of(phase, period):
    wrapped = phase & (period - 1)
    folded = jnp.minimum(wrapped, period - wrapped)
    flip = folded > period // 4
    folded = jnp.where(flip, period // 2 - folded, folded)
    x = folded.astype(jnp.float32) * (2.0 * math.pi / period)
    y = x * x
    value = jnp.full_like(y, 1.0 / math.factorial(16))
    for n in range(14, -1, -2):
        sign = -1.0 if n % 4 else 1.0
        value = value * y + sign / math.factorial(n)
    return jnp.where(flip, -value, value)


def fused_kernel(
    nb, nm, vel_hbm, modes_hbm, res_hbm, rank_hbm, freq_hbm, out_ref,
    vel_ref, modes_ref, res_ref, rank_ref, freq_ref,
    table, trig, modes_t, res_t, spec, part, pend, summed, coef, force, basis, acc,
    ready, in_s, tx, sx_r, sm_r, sf_r, ry_r, rz_r, k_r, ob_r,
    far_r, nu_r, nl_r, cu_r, cl_r, g_r, h_r, mf_r,
):
    b = lax.axis_index("band")
    m = lax.axis_index("mode")
    mate = m + 1 - 2 * (m % 2)
    cross = (m + 2) % nm
    here = m // 2
    patches, steps = vel_ref.shape
    cols = table.shape[2]
    mode_cols = modes_ref.shape[1]
    pairs = nb // 2
    inner = (b // 2 + 1) // 2 % 2

    def band_at(e):
        bits = [1 << i for i in range(nb.bit_length() - 1)]
        return sum(bit * ((b // bit + e // bit) % 2) for bit in bits)

    near = band_at(1)

    def to_mode(src, dst, send, recv, target):
        return pltpu.make_async_remote_copy(
            src_ref=src, dst_ref=dst, send_sem=tx.at[send], recv_sem=recv,
            device_id={"mode": target}, device_id_type=MESH)

    def to_band(src, dst, send, recv, target):
        return pltpu.make_async_remote_copy(
            src_ref=src, dst_ref=dst, send_sem=tx.at[send], recv_sem=recv,
            device_id={"band": target}, device_id_type=MESH)

    def wait_bytes(ref, sem):
        pltpu.make_async_copy(ref, ref, sem).wait()

    loads = [
        pltpu.make_async_copy(src, dst, in_s.at[i])
        for i, (src, dst) in enumerate((
            (freq_hbm, freq_ref), (vel_hbm, vel_ref), (modes_hbm, modes_ref),
            (res_hbm, res_ref), (rank_hbm, rank_ref)))
    ]
    for load in loads:
        load.start()
    barrier = pltpu.get_barrier_semaphore()
    for off in range(1, nm):
        pl.semaphore_signal(barrier, inc=1, device_id={"mode": (m + off) % nm}, device_id_type=MESH)
    for off in (1, 2):
        pl.semaphore_signal(barrier, inc=1, device_id={"band": band_at(off)}, device_id_type=MESH)

    @pl.when(inner == 1)
    def _():
        pl.semaphore_signal(barrier, inc=1, device_id={"band": band_at(6)}, device_id_type=MESH)

    blocks = steps // HALF_ROWS
    norming = 1.0 / math.sqrt(steps)

    def build(k):
        half = cols // 2
        lane = lax.broadcasted_iota(jnp.int32, (HALF_ROWS, cols), 1)
        row = jnp.broadcast_to(freq_ref[pl.ds(k // 2, 1), :], (HALF_ROWS, cols))
        freq = jnp.where(lane // half == k % 2, row, pltpu.roll(row, half, 1))
        shift = jnp.where(lane < half, 0, steps // 4)
        rows = lax.broadcasted_iota(jnp.int32, (HALF_ROWS, cols), 0)
        big = lax.broadcasted_iota(jnp.int32, (blocks, cols), 0) * HALF_ROWS
        low = rows * freq + shift
        high = big * freq
        quarter = steps // 4
        cos_low = cosine_of(low, steps) * norming
        sin_low = cosine_of(low - quarter, steps) * norming
        trig[0] = cosine_of(high, steps)
        trig[1] = cosine_of(high - quarter, steps)
        for a in range(blocks):
            row = trig[0, pl.ds(a, 1), :] * cos_low - trig[1, pl.ds(a, 1), :] * sin_low
            table[k, pl.ds(a * HALF_ROWS, HALF_ROWS), :] = row.astype(jnp.bfloat16)

    def project(k):
        spec[k, m] = jnp.dot(
            vel_ref[...], table[k], preferred_element_type=jnp.float32
        ).astype(jnp.bfloat16)

    order = (7, 5, 6, 3, 4, 1, 2, 0)

    def slot(i):
        return band_at(order[i])

    def s_cross(k):
        return to_mode(spec.at[k, m], spec.at[k, m], 0, sx_r.at[k], cross)

    def s_mate(k):
        return to_mode(spec.at[k, m], spec.at[k, m], 0, sm_r.at[0], mate)

    def s_fwd(k):
        return to_mode(spec.at[k, cross], spec.at[k, cross], 0, sf_r.at[k], mate)

    loads[0].wait()
    build(slot(0))
    loads[1].wait()
    project(slot(0))
    pl.semaphore_wait(barrier, nm + 1 + inner)

    @pl.when(inner == 1)
    def _():
        pl.semaphore_signal(ready, inc=1, device_id={"band": band_at(6)}, device_id_type=MESH)

    for i in range(nb):
        s_cross(slot(i)).start()
        s_mate(slot(i)).start()
        if i < nb - 1:
            build(slot(i + 1))
            project(slot(i + 1))

    def basis_copy(off):
        target = (m + off) % nm
        rows = pl.ds(pl.multiple_of(target * patches, patches), patches)
        return to_mode(modes_ref.at[rows], basis.at[m], 3, ob_r.at[0], target)

    loads[2].wait()
    for off in range(1, nm):
        basis_copy(off).start()

    @pl.when(inner == 1)
    def _():
        pl.semaphore_wait(ready, 1)
        pl.semaphore_signal(ready, inc=1, device_id={"band": band_at(2)}, device_id_type=MESH)

    for half in range(2):
        rows = pl.ds(pl.multiple_of(((here + half) % 2) * 2 * patches, 2 * patches), 2 * patches)
        modes_t[half] = modes_ref[rows, :].T
    wait_bytes(spec.at[pl.ds(0, nb // nm)], sm_r.at[0])

    def partial(k, half):
        chip = pl.ds(pl.multiple_of(((here + half) % 2) * 2, 2), 2)
        return jnp.dot(
            modes_t[half], spec[k, chip].reshape(2 * patches, cols), preferred_element_type=jnp.float32)

    def y_copy(j):
        return to_band(part.at[2 * j + 1], summed.at[j], 1, ry_r.at[j], near)

    def z_copy(j):
        return to_band(part.at[2 * j], summed.at[pairs + j - 1], 1, rz_r.at[j - 1], band_at(2 * j))

    def pass_on(j, value):
        y_copy(j).wait_recv()
        part[2 * j] = (value + summed[j].astype(jnp.float32)).astype(jnp.bfloat16)
        z_copy(j).start()

    for i, e in enumerate(order):
        k = slot(i)
        own = partial(k, 0)
        s_cross(k).wait_recv()
        s_fwd(k).start()
        if e == 3:
            @pl.when(inner == 0)
            def _():
                pl.semaphore_wait(ready, 1)

            pass_on(3, pend[...])
        s_fwd(k).wait_recv()
        value = own + partial(k, 1)
        if e % 2:
            part[e] = value.astype(jnp.bfloat16)
            y_copy(e // 2).start()
        elif e == 6:
            pend[...] = value
        elif e:
            pass_on(e // 2, value)
        else:
            pend[...] = value
    loads[3].wait()
    res_t[...] = res_ref[...].astype(jnp.bfloat16).T
    loads[4].wait()
    total = pend[...]
    for j in range(pairs - 1, 0, -1):
        z_copy(j).wait_recv()
        total = total + summed[pairs + j - 1].astype(jnp.float32)
    y_copy(0).wait_recv()
    total = total + summed[0].astype(jnp.float32)
    kept = lax.broadcasted_iota(jnp.int32, (mode_cols, cols), 0) + m * mode_cols < rank_ref[...]
    total = jnp.where(kept, total, 0.0)
    coef[m] = total.astype(jnp.bfloat16)

    split = mode_cols * 5 // 8 // 16 * 16
    head, tail = pl.ds(0, split), pl.ds(split, mode_cols - split)

    def k_copy(source, rows, sem, target):
        piece = coef.at[source, rows]
        return to_mode(piece, piece, 2, k_r.at[sem], target)

    k_copy(m, head, 0, cross).start()
    k_copy(m, tail, 1, cross).start()
    k_copy(m, tail, 2, (mate + 2) % nm).start()
    k_copy(m, head, 3, mate).start()
    k_copy(m, tail, 4, mate).start()
    k_copy(cross, head, 0, cross).wait_recv()
    k_copy(cross, head, 5, mate).start()
    for rows, sem in ((tail, 1), (tail, 2), (head, 3), (tail, 4), (head, 5)):
        k_copy(m, rows, sem, mate).wait_recv()
    coefs = coef[...].reshape(nm * mode_cols, cols)
    forcing = jnp.dot(res_t[...], coefs, preferred_element_type=jnp.float32)
    forcing = jnp.where(kept, 2.0 * forcing, 0.0)
    force[b, m] = forcing.astype(jnp.bfloat16)

    half = mode_cols // 2
    upper, lower = pl.ds(0, half), pl.ds(half, half)

    def f_far(j):
        piece = force.at[b, m]
        return to_band(piece, piece, 5, far_r.at[j - 1], band_at(2 * j))

    def f_near(j, rows, sem):
        piece = force.at[band_at(2 * j), m, rows]
        return to_band(piece, piece, 4, sem.at[j], near)

    def f_cross(j, rows, sem):
        piece = force.at[band_at(2 * j), m, rows]
        return to_mode(piece, piece, 4, sem.at[j], cross)

    def g_near(j):
        piece = force.at[band_at(2 * j), cross, lower]
        return to_band(piece, piece, 4, g_r.at[j], near)

    def g_cross(j):
        piece = force.at[band_at(2 * j + 1), m, upper]
        return to_mode(piece, piece, 4, g_r.at[j], cross)

    def f_diag(j):
        piece = force.at[band_at(2 * j), m]
        return pltpu.make_async_remote_copy(
            src_ref=piece, dst_ref=piece, send_sem=tx.at[4], recv_sem=g_r.at[j],
            device_id={"band": near, "mode": cross}, device_id_type=MESH)

    def h_near():
        piece = force.at[near, m]
        return to_band(piece, piece, 4, h_r.at[0], band_at(2))

    def h_cross():
        piece = force.at[b, cross]
        return to_band(piece, piece, 4, h_r.at[1], band_at(2))

    def f_mate(e):
        piece = force.at[band_at(e), m]
        return to_mode(piece, piece, 4, mf_r.at[e], mate)

    def f_fwd(e):
        piece = force.at[band_at(e), cross]
        return to_mode(piece, piece, 4, mf_r.at[e], mate)

    def arrived(j):
        f_far(j).wait_recv()

    whole = pl.ds(0, mode_cols)

    def first(j):
        if j == 0:
            f_near(j, whole, nl_r).start()
            f_cross(j, whole, cu_r).start()
        elif j != 1:
            f_near(j, upper, nu_r).start()
            f_cross(j, lower, cl_r).start()
            f_near(j, lower, nl_r).start()
            f_cross(j, upper, cu_r).start()
        f_mate(2 * j).start()

    def second(j):
        if j == 1:
            h_near().wait_recv()
            g_cross(j).start()
            f_mate(2 * j + 1).start()
            h_cross().wait_recv()
            g_near(j).start()
            f_fwd(2 * j).start()
            return
        f_near(j, upper, nu_r).wait_recv()
        if j:
            g_cross(j).start()
        f_cross(j, lower, cl_r).wait_recv()
        if j:
            g_near(j).start()

    def late():
        @pl.when(inner == 1)
        def _():
            f_far(3).start()

    def settle(j):
        rows_n, rows_c = (lower, upper) if j else (whole, whole)
        f_near(j, rows_n, nl_r).wait_recv()
        if j == 0:
            late()
            h_near().start()
        f_mate(2 * j + 1).start()
        f_cross(j, rows_c, cu_r).wait_recv()
        if j == 0:
            h_cross().start()
        f_fwd(2 * j).start()

    def third(j):
        wait_bytes(force.at[0, 0], g_r.at[j])
        f_fwd(2 * j + 1).start()

    first(0)
    f_diag(0).start()
    f_far(1).start()
    f_far(3 - inner).start()

    @pl.when(inner == 0)
    def _():
        f_far(2).start()


    wait_bytes(basis.at[pl.ds(0, nm - 1)], ob_r.at[0])
    basis[m] = modes_ref[pl.ds(pl.multiple_of(m * patches, patches), patches), :]

    def surface(k):
        value = jnp.dot(basis[0], force[k, 0], preferred_element_type=jnp.float32)
        for j in range(1, nm):
            value = value + jnp.dot(basis[j], force[k, j], preferred_element_type=jnp.float32)
        return value.astype(jnp.bfloat16)

    def last(e, place=1):
        k = band_at(e)
        wait_bytes(force.at[0, pl.ds(0, 2)], mf_r.at[e])
        term = lax.dot_general(
            surface(k), table[k], (((1,), (1,)), ((), ())), preferred_element_type=jnp.float32)
        if place == 0:
            acc[...] = term
        elif place == 1:
            acc[...] += term
        else:
            out_ref[...] = (acc[...] + term).astype(out_ref.dtype)

    settle(0)
    arrived(2)
    first(2)
    arrived(1)
    first(1)
    third(0)
    last(0, 0)
    arrived(3)
    first(3)
    last(1, 1)
    second(2)
    settle(2)
    second(1)
    second(3)
    settle(3)
    third(2)
    last(4, 1)
    last(2, 1)
    third(1)
    last(6, 1)
    third(3)
    last(5, 1)
    last(3, 1)
    last(7, 2)

    wait_bytes(spec.at[pl.ds(0, nb - nb // nm)], tx.at[0])
    wait_bytes(part.at[pl.ds(0, nb - 1)], tx.at[1])
    wait_bytes(coef.at[pl.ds(0, nm - 1)], tx.at[2])
    wait_bytes(basis.at[pl.ds(0, nm - 1)], tx.at[3])
    wait_bytes(force.at[pl.ds(0, nb - 1)], tx.at[4])
    wait_bytes(force.at[0, pl.ds(0, pairs - 1)], tx.at[5])


def fused(mesh, velocity, radiation_modes, resistance, mode_ranks, freq_table):
    nb, nm = mesh.shape["band"], mesh.shape["mode"]
    patches, steps = velocity.shape[1:]
    mode_cols = radiation_modes.shape[1]
    modes = nm * mode_cols
    cols = 2 * (freq_table.shape[0] // nb)
    pairs = nb // 2
    bf16, f32 = jnp.bfloat16, jnp.float32
    sems = (5, 6, nb, 1, nb, pairs, pairs - 1, 6, 1, pairs - 1, pairs, pairs, pairs, pairs, pairs, 2, nb)
    hbm = pl.BlockSpec(memory_space=pltpu.HBM)
    out = pl.pallas_call(
        functools.partial(fused_kernel, nb, nm),
        out_shape=pltpu.VMEM((patches, steps), bf16),
        in_specs=[hbm] * 5,
        out_specs=pl.BlockSpec(memory_space=pltpu.VMEM),
        scratch_shapes=[
            pltpu.VMEM((patches, steps), bf16),
            pltpu.VMEM(radiation_modes.shape, bf16),
            pltpu.VMEM(resistance.shape[1:], f32),
            pltpu.VMEM((1, 1), jnp.int32),
            pltpu.VMEM((pairs, cols), jnp.int32),
            pltpu.VMEM((nb, steps, cols), bf16),
            pltpu.VMEM((2, steps // HALF_ROWS, cols), f32),
            pltpu.VMEM((2, mode_cols, 2 * patches), bf16),
            pltpu.VMEM((mode_cols, modes), bf16),
            pltpu.VMEM((nb, nm, patches, cols), bf16),
            pltpu.VMEM((nb, mode_cols, cols), bf16),
            pltpu.VMEM((mode_cols, cols), f32),
            pltpu.VMEM((nb - 1, mode_cols, cols), bf16),
            pltpu.VMEM((nm, mode_cols, cols), bf16),
            pltpu.VMEM((nb, nm, mode_cols, cols), bf16),
            pltpu.VMEM((nm, patches, mode_cols), bf16),
            pltpu.VMEM((patches, steps), f32),
        ]
        + [pltpu.SemaphoreType.REGULAR]
        + [pltpu.SemaphoreType.DMA((n,)) for n in sems],
        compiler_params=pltpu.CompilerParams(collective_id=0, has_side_effects=True),
    )(velocity[0], radiation_modes, resistance[0], mode_ranks.reshape(1, 1), freq_table.reshape(pairs, cols))
    return out[None]


def make_table(freq_table, step_count):
    times = jnp.arange(step_count, dtype=jnp.int32)
    phases = times[:, None] * freq_table[None, :] % step_count
    angles = phases.astype(jnp.float32) * (2.0 * math.pi / step_count)
    norming = 1.0 / math.sqrt(step_count)
    table = jnp.stack([jnp.cos(angles), -jnp.sin(angles)], axis=1) * norming
    return table.astype(jnp.bfloat16)


def add_sources(received):
    return jnp.sum(received, axis=0)


def per_device(velocity, radiation_modes, resistance, mode_ranks, freq_table):
    step_count = velocity.shape[2]
    mode_cols = radiation_modes.shape[1]
    dft_table = make_table(freq_table, step_count)
    spectra = jnp.einsum(
        "wpt,tcf->wpcf", velocity, dft_table, preferred_element_type=jnp.float32
    ).astype(jnp.bfloat16)
    partial_value = jnp.einsum(
        "wpcf,pr->wrcf",
        lax.all_gather(spectra, "mode", axis=1, tiled=True),
        radiation_modes,
        preferred_element_type=jnp.float32,
    )
    coefficients = add_sources(
        lax.all_to_all(
            partial_value[None].astype(jnp.bfloat16),
            "band",
            split_axis=4,
            concat_axis=0,
            tiled=True,
        ).astype(jnp.float32)
    )
    offset = lax.axis_index("mode") * mode_cols
    rank_here = mode_ranks[0]
    kept_mask = (offset + jnp.arange(mode_cols, dtype=jnp.int32) < rank_here).astype(jnp.float32)
    kept_mask = kept_mask[None, :, None, None]
    coefficients = coefficients * kept_mask
    matrix = resistance[0]
    partial_terms = jnp.einsum(
        "ij,wjcf->wicf", matrix, coefficients, precision=lax.Precision.HIGHEST
    )
    forcing = lax.psum_scatter(
        partial_terms.astype(jnp.bfloat16), "mode", scatter_dimension=1, tiled=True
    ).astype(jnp.float32)
    forcing = (2.0 * forcing * kept_mask).astype(jnp.bfloat16)
    collected = lax.all_gather(forcing, "mode", axis=1, tiled=True)
    collected = lax.all_gather(collected, "band", axis=3, tiled=True)
    own_basis = lax.all_to_all(radiation_modes, "mode", split_axis=0, concat_axis=1, tiled=True)
    surface_force = jnp.einsum(
        "pr,wrcf->wpcf", own_basis, collected, preferred_element_type=jnp.float32
    ).astype(jnp.bfloat16)
    history = jnp.einsum(
        "wpcf,tcf->wpt", surface_force, dft_table, preferred_element_type=jnp.float32
    )
    return history.astype(jnp.bfloat16)


def solution(mesh):
    placed = (
        P(None, ("band", "mode"), None),
        P("band", "mode"),
        P("band", None, "mode"),
        P("band"),
        P(),
    )
    nb, nm = mesh.shape["band"], mesh.shape["mode"]

    def body(velocity, radiation_modes, resistance, mode_ranks, freq_table):
        windows, patches, steps = velocity.shape
        mode_cols = radiation_modes.shape[1]
        cols = 2 * (freq_table.shape[0] // nb)
        tiled = (
            windows == 1 and nm == 4 and nb == 8 and cols == 128 and mode_cols % 128 == 0
            and patches % 128 == 0 and steps % 128 == 0 and steps & (steps - 1) == 0
        )
        args = (velocity, radiation_modes, resistance, mode_ranks, freq_table)
        return fused(mesh, *args) if tiled else per_device(*args)

    return jax.shard_map(
        body,
        mesh=mesh,
        in_specs=placed,
        out_specs=P(None, ("band", "mode"), None),
        check_vma=False,
    )
```

```python
import functools
import math

import jax
import jax.numpy as jnp
from jax import lax
from jax.experimental import pallas as pl
from jax.experimental.pallas import tpu as pltpu
from jax.sharding import PartitionSpec as P

MESH = pl.DeviceIdType.MESH
HALF_ROWS = 32


def cosine_of(phase, period):
    wrapped = phase & (period - 1)
    folded = jnp.minimum(wrapped, period - wrapped)
    flip = folded > period // 4
    folded = jnp.where(flip, period // 2 - folded, folded)
    x = folded.astype(jnp.float32) * (2.0 * math.pi / period)
    y = x * x
    value = jnp.full_like(y, 1.0 / math.factorial(16))
    for n in range(14, -1, -2):
        sign = -1.0 if n % 4 else 1.0
        value = value * y + sign / math.factorial(n)
    return jnp.where(flip, -value, value)


def fused_kernel(
    nb, nm, vel_hbm, modes_hbm, res_hbm, rank_hbm, freq_hbm, out_ref,
    vel_ref, modes_ref, res_ref, rank_ref, freq_ref,
    table, trig, modes_t, res_t, spec, part, pend, summed, coef, force, basis, acc,
    ready, in_s, tx, sx_r, sm_r, sf_r, ry_r, rz_r, k_r, ob_r,
    far_r, nu_r, nl_r, cu_r, cl_r, g_r, h_r, mf_r,
):
    b = lax.axis_index("band")
    m = lax.axis_index("mode")
    mate = m + 1 - 2 * (m % 2)
    cross = (m + 2) % nm
    here = m // 2
    patches, steps = vel_ref.shape
    cols = table.shape[2]
    mode_cols = modes_ref.shape[1]
    pairs = nb // 2
    inner = (b // 2 + 1) // 2 % 2

    def band_at(e):
        bits = [1 << i for i in range(nb.bit_length() - 1)]
        return sum(bit * ((b // bit + e // bit) % 2) for bit in bits)

    near = band_at(1)

    def to_mode(src, dst, send, recv, target):
        return pltpu.make_async_remote_copy(
            src_ref=src, dst_ref=dst, send_sem=tx.at[send], recv_sem=recv,
            device_id={"mode": target}, device_id_type=MESH)

    def to_band(src, dst, send, recv, target):
        return pltpu.make_async_remote_copy(
            src_ref=src, dst_ref=dst, send_sem=tx.at[send], recv_sem=recv,
            device_id={"band": target}, device_id_type=MESH)

    def wait_bytes(ref, sem):
        pltpu.make_async_copy(ref, ref, sem).wait()

    loads = [
        pltpu.make_async_copy(src, dst, in_s.at[i])
        for i, (src, dst) in enumerate((
            (freq_hbm, freq_ref), (vel_hbm, vel_ref), (modes_hbm, modes_ref),
            (res_hbm, res_ref), (rank_hbm, rank_ref)))
    ]
    for load in loads:
        load.start()
    barrier = pltpu.get_barrier_semaphore()
    for off in range(1, nm):
        pl.semaphore_signal(barrier, inc=1, device_id={"mode": (m + off) % nm}, device_id_type=MESH)
    for off in (1, 2):
        pl.semaphore_signal(barrier, inc=1, device_id={"band": band_at(off)}, device_id_type=MESH)

    @pl.when(inner == 1)
    def _():
        pl.semaphore_signal(barrier, inc=1, device_id={"band": band_at(6)}, device_id_type=MESH)

    blocks = steps // HALF_ROWS
    norming = 1.0 / math.sqrt(steps)

    def build(k):
        half = cols // 2
        lane = lax.broadcasted_iota(jnp.int32, (HALF_ROWS, cols), 1)
        row = jnp.broadcast_to(freq_ref[pl.ds(k // 2, 1), :], (HALF_ROWS, cols))
        freq = jnp.where(lane // half == k % 2, row, pltpu.roll(row, half, 1))
        shift = jnp.where(lane < half, 0, steps // 4)
        rows = lax.broadcasted_iota(jnp.int32, (HALF_ROWS, cols), 0)
        big = lax.broadcasted_iota(jnp.int32, (blocks, cols), 0) * HALF_ROWS
        low = rows * freq + shift
        high = big * freq
        quarter = steps // 4
        cos_low = cosine_of(low, steps) * norming
        sin_low = cosine_of(low - quarter, steps) * norming
        trig[0] = cosine_of(high, steps)
        trig[1] = cosine_of(high - quarter, steps)
        for a in range(blocks):
            row = trig[0, pl.ds(a, 1), :] * cos_low - trig[1, pl.ds(a, 1), :] * sin_low
            table[k, pl.ds(a * HALF_ROWS, HALF_ROWS), :] = row.astype(jnp.bfloat16)

    def project(k):
        spec[k, m] = jnp.dot(
            vel_ref[...], table[k], preferred_element_type=jnp.float32
        ).astype(jnp.bfloat16)

    order = (7, 5, 6, 3, 4, 1, 2, 0)

    def slot(i):
        return band_at(order[i])

    def s_cross(k):
        return to_mode(spec.at[k, m], spec.at[k, m], 0, sx_r.at[k], cross)

    def s_mate(k):
        return to_mode(spec.at[k, m], spec.at[k, m], 0, sm_r.at[0], mate)

    def s_fwd(k):
        return to_mode(spec.at[k, cross], spec.at[k, cross], 0, sf_r.at[k], mate)

    loads[0].wait()
    build(slot(0))
    loads[1].wait()
    project(slot(0))
    pl.semaphore_wait(barrier, nm + 1 + inner)

    @pl.when(inner == 1)
    def _():
        pl.semaphore_signal(ready, inc=1, device_id={"band": band_at(6)}, device_id_type=MESH)

    for i in range(nb):
        s_cross(slot(i)).start()
        s_mate(slot(i)).start()
        if i < nb - 1:
            build(slot(i + 1))
            project(slot(i + 1))

    def basis_copy(off):
        target = (m + off) % nm
        rows = pl.ds(pl.multiple_of(target * patches, patches), patches)
        return to_mode(modes_ref.at[rows], basis.at[m], 3, ob_r.at[0], target)

    loads[2].wait()
    for off in range(1, nm):
        basis_copy(off).start()

    @pl.when(inner == 1)
    def _():
        pl.semaphore_wait(ready, 1)
        pl.semaphore_signal(ready, inc=1, device_id={"band": band_at(2)}, device_id_type=MESH)

    for half in range(2):
        rows = pl.ds(pl.multiple_of(((here + half) % 2) * 2 * patches, 2 * patches), 2 * patches)
        modes_t[half] = modes_ref[rows, :].T
    wait_bytes(spec.at[pl.ds(0, nb // nm)], sm_r.at[0])

    def partial(k, half):
        chip = pl.ds(pl.multiple_of(((here + half) % 2) * 2, 2), 2)
        return jnp.dot(
            modes_t[half], spec[k, chip].reshape(2 * patches, cols), preferred_element_type=jnp.float32)

    def y_copy(j):
        return to_band(part.at[2 * j + 1], summed.at[j], 1, ry_r.at[j], near)

    def z_copy(j):
        return to_band(part.at[2 * j], summed.at[pairs + j - 1], 1, rz_r.at[j - 1], band_at(2 * j))

    def pass_on(j, value):
        y_copy(j).wait_recv()
        part[2 * j] = (value + summed[j].astype(jnp.float32)).astype(jnp.bfloat16)
        z_copy(j).start()

    for i, e in enumerate(order):
        k = slot(i)
        own = partial(k, 0)
        s_cross(k).wait_recv()
        s_fwd(k).start()
        if e == 3:
            @pl.when(inner == 0)
            def _():
                pl.semaphore_wait(ready, 1)

            pass_on(3, pend[...])
        s_fwd(k).wait_recv()
        value = own + partial(k, 1)
        if e % 2:
            part[e] = value.astype(jnp.bfloat16)
            y_copy(e // 2).start()
        elif e == 6:
            pend[...] = value
        elif e:
            pass_on(e // 2, value)
        else:
            pend[...] = value
    loads[3].wait()
    res_t[...] = res_ref[...].astype(jnp.bfloat16).T
    loads[4].wait()
    total = pend[...]
    for j in range(pairs - 1, 0, -1):
        z_copy(j).wait_recv()
        total = total + summed[pairs + j - 1].astype(jnp.float32)
    y_copy(0).wait_recv()
    total = total + summed[0].astype(jnp.float32)
    kept = lax.broadcasted_iota(jnp.int32, (mode_cols, cols), 0) + m * mode_cols < rank_ref[...]
    total = jnp.where(kept, total, 0.0)
    coef[m] = total.astype(jnp.bfloat16)

    split = mode_cols * 5 // 8 // 16 * 16
    head, tail = pl.ds(0, split), pl.ds(split, mode_cols - split)

    def k_copy(source, rows, sem, target):
        piece = coef.at[source, rows]
        return to_mode(piece, piece, 2, k_r.at[sem], target)

    k_copy(m, head, 0, cross).start()
    k_copy(m, tail, 1, cross).start()
    k_copy(m, tail, 2, (mate + 2) % nm).start()
    k_copy(m, head, 3, mate).start()
    k_copy(m, tail, 4, mate).start()
    k_copy(cross, head, 0, cross).wait_recv()
    k_copy(cross, head, 5, mate).start()
    for rows, sem in ((tail, 1), (tail, 2), (head, 3), (tail, 4), (head, 5)):
        k_copy(m, rows, sem, mate).wait_recv()
    coefs = coef[...].reshape(nm * mode_cols, cols)
    forcing = jnp.dot(res_t[...], coefs, preferred_element_type=jnp.float32)
    forcing = jnp.where(kept, 2.0 * forcing, 0.0)
    force[b, m] = forcing.astype(jnp.bfloat16)

    half = mode_cols // 2
    upper, lower = pl.ds(0, half), pl.ds(half, half)

    def f_far(j, rows=pl.ds(0, mode_cols)):
        piece = force.at[b, m, rows]
        return to_band(piece, piece, 5, far_r.at[j - 1], band_at(2 * j))

    def f_near(j, rows, sem):
        piece = force.at[band_at(2 * j), m, rows]
        return to_band(piece, piece, 4, sem.at[j], near)

    def f_cross(j, rows, sem):
        piece = force.at[band_at(2 * j), m, rows]
        return to_mode(piece, piece, 4, sem.at[j], cross)

    def g_near(j):
        piece = force.at[band_at(2 * j), cross, lower]
        return to_band(piece, piece, 4, g_r.at[j], near)

    def g_cross(j):
        piece = force.at[band_at(2 * j + 1), m, upper]
        return to_mode(piece, piece, 4, g_r.at[j], cross)

    def f_diag(j):
        piece = force.at[band_at(2 * j), m]
        return pltpu.make_async_remote_copy(
            src_ref=piece, dst_ref=piece, send_sem=tx.at[4], recv_sem=g_r.at[j],
            device_id={"band": near, "mode": cross}, device_id_type=MESH)

    def h_near():
        piece = force.at[near, m]
        return to_band(piece, piece, 4, h_r.at[0], band_at(2))

    def h_cross():
        piece = force.at[b, cross]
        return to_band(piece, piece, 4, h_r.at[1], band_at(2))

    def f_mate(e):
        piece = force.at[band_at(e), m]
        return to_mode(piece, piece, 4, mf_r.at[e], mate)

    def f_fwd(e):
        piece = force.at[band_at(e), cross]
        return to_mode(piece, piece, 4, mf_r.at[e], mate)

    def arrived(j):
        f_far(j).wait_recv()

    def first(j):
        if j != 1:
            f_near(j, upper, nu_r).start()
            f_cross(j, lower, cl_r).start()
            f_near(j, lower, nl_r).start()
            f_cross(j, upper, cu_r).start()
        f_mate(2 * j).start()

    def second(j):
        if j == 1:
            h_near().wait_recv()
            g_cross(j).start()
            f_mate(2 * j + 1).start()
            h_cross().wait_recv()
            g_near(j).start()
            f_fwd(2 * j).start()
            return
        f_near(j, upper, nu_r).wait_recv()
        if j:
            g_cross(j).start()
        f_cross(j, lower, cl_r).wait_recv()
        if j:
            g_near(j).start()

    def settle(j):
        f_near(j, lower, nl_r).wait_recv()
        if j == 0:
            h_near().start()
        f_mate(2 * j + 1).start()
        f_cross(j, upper, cu_r).wait_recv()
        if j == 0:
            h_cross().start()
        f_fwd(2 * j).start()

    def third(j):
        wait_bytes(force.at[0, 0], g_r.at[j])
        f_fwd(2 * j + 1).start()

    first(0)
    f_diag(0).start()
    f_far(1).start()
    f_far(3 - inner).start()

    @pl.when(inner == 0)
    def _():
        f_far(2).start()


    @pl.when(inner == 1)
    def _():
        f_far(3, upper).start()

    wait_bytes(basis.at[pl.ds(0, nm - 1)], ob_r.at[0])
    basis[m] = modes_ref[pl.ds(pl.multiple_of(m * patches, patches), patches), :]

    def surface(k):
        value = jnp.dot(basis[0], force[k, 0], preferred_element_type=jnp.float32)
        for j in range(1, nm):
            value = value + jnp.dot(basis[j], force[k, j], preferred_element_type=jnp.float32)
        return value.astype(jnp.bfloat16)

    def last(e, place=1):
        k = band_at(e)
        wait_bytes(force.at[0, pl.ds(0, 2)], mf_r.at[e])
        term = lax.dot_general(
            surface(k), table[k], (((1,), (1,)), ((), ())), preferred_element_type=jnp.float32)
        if place == 0:
            acc[...] = term
        elif place == 1:
            acc[...] += term
        else:
            out_ref[...] = (acc[...] + term).astype(out_ref.dtype)

    second(0)

    @pl.when(inner == 1)
    def _():
        f_far(3, lower).start()

    settle(0)
    arrived(1)
    first(1)
    arrived(2)
    first(2)
    third(0)
    last(0, 0)
    arrived(3)
    first(3)
    last(1, 1)
    second(2)
    settle(2)
    second(1)
    second(3)
    settle(3)
    third(2)
    last(4, 1)
    last(2, 1)
    third(1)
    last(6, 1)
    third(3)
    last(5, 1)
    last(3, 1)
    last(7, 2)

    wait_bytes(spec.at[pl.ds(0, nb - nb // nm)], tx.at[0])
    wait_bytes(part.at[pl.ds(0, nb - 1)], tx.at[1])
    wait_bytes(coef.at[pl.ds(0, nm - 1)], tx.at[2])
    wait_bytes(basis.at[pl.ds(0, nm - 1)], tx.at[3])
    wait_bytes(force.at[pl.ds(0, nb - 1)], tx.at[4])
    wait_bytes(force.at[0, pl.ds(0, pairs - 1)], tx.at[5])


def fused(mesh, velocity, radiation_modes, resistance, mode_ranks, freq_table):
    nb, nm = mesh.shape["band"], mesh.shape["mode"]
    patches, steps = velocity.shape[1:]
    mode_cols = radiation_modes.shape[1]
    modes = nm * mode_cols
    cols = 2 * (freq_table.shape[0] // nb)
    pairs = nb // 2
    bf16, f32 = jnp.bfloat16, jnp.float32
    sems = (5, 6, nb, 1, nb, pairs, pairs - 1, 6, 1, pairs - 1, pairs, pairs, pairs, pairs, pairs, 2, nb)
    hbm = pl.BlockSpec(memory_space=pltpu.HBM)
    out = pl.pallas_call(
        functools.partial(fused_kernel, nb, nm),
        out_shape=pltpu.VMEM((patches, steps), bf16),
        in_specs=[hbm] * 5,
        out_specs=pl.BlockSpec(memory_space=pltpu.VMEM),
        scratch_shapes=[
            pltpu.VMEM((patches, steps), bf16),
            pltpu.VMEM(radiation_modes.shape, bf16),
            pltpu.VMEM(resistance.shape[1:], f32),
            pltpu.VMEM((1, 1), jnp.int32),
            pltpu.VMEM((pairs, cols), jnp.int32),
            pltpu.VMEM((nb, steps, cols), bf16),
            pltpu.VMEM((2, steps // HALF_ROWS, cols), f32),
            pltpu.VMEM((2, mode_cols, 2 * patches), bf16),
            pltpu.VMEM((mode_cols, modes), bf16),
            pltpu.VMEM((nb, nm, patches, cols), bf16),
            pltpu.VMEM((nb, mode_cols, cols), bf16),
            pltpu.VMEM((mode_cols, cols), f32),
            pltpu.VMEM((nb - 1, mode_cols, cols), bf16),
            pltpu.VMEM((nm, mode_cols, cols), bf16),
            pltpu.VMEM((nb, nm, mode_cols, cols), bf16),
            pltpu.VMEM((nm, patches, mode_cols), bf16),
            pltpu.VMEM((patches, steps), f32),
        ]
        + [pltpu.SemaphoreType.REGULAR]
        + [pltpu.SemaphoreType.DMA((n,)) for n in sems],
        compiler_params=pltpu.CompilerParams(collective_id=0, has_side_effects=True),
    )(velocity[0], radiation_modes, resistance[0], mode_ranks.reshape(1, 1), freq_table.reshape(pairs, cols))
    return out[None]


def make_table(freq_table, step_count):
    times = jnp.arange(step_count, dtype=jnp.int32)
    phases = times[:, None] * freq_table[None, :] % step_count
    angles = phases.astype(jnp.float32) * (2.0 * math.pi / step_count)
    norming = 1.0 / math.sqrt(step_count)
    table = jnp.stack([jnp.cos(angles), -jnp.sin(angles)], axis=1) * norming
    return table.astype(jnp.bfloat16)


def add_sources(received):
    return jnp.sum(received, axis=0)


def per_device(velocity, radiation_modes, resistance, mode_ranks, freq_table):
    step_count = velocity.shape[2]
    mode_cols = radiation_modes.shape[1]
    dft_table = make_table(freq_table, step_count)
    spectra = jnp.einsum(
        "wpt,tcf->wpcf", velocity, dft_table, preferred_element_type=jnp.float32
    ).astype(jnp.bfloat16)
    partial_value = jnp.einsum(
        "wpcf,pr->wrcf",
        lax.all_gather(spectra, "mode", axis=1, tiled=True),
        radiation_modes,
        preferred_element_type=jnp.float32,
    )
    coefficients = add_sources(
        lax.all_to_all(
            partial_value[None].astype(jnp.bfloat16),
            "band",
            split_axis=4,
            concat_axis=0,
            tiled=True,
        ).astype(jnp.float32)
    )
    offset = lax.axis_index("mode") * mode_cols
    rank_here = mode_ranks[0]
    kept_mask = (offset + jnp.arange(mode_cols, dtype=jnp.int32) < rank_here).astype(jnp.float32)
    kept_mask = kept_mask[None, :, None, None]
    coefficients = coefficients * kept_mask
    matrix = resistance[0]
    partial_terms = jnp.einsum(
        "ij,wjcf->wicf", matrix, coefficients, precision=lax.Precision.HIGHEST
    )
    forcing = lax.psum_scatter(
        partial_terms.astype(jnp.bfloat16), "mode", scatter_dimension=1, tiled=True
    ).astype(jnp.float32)
    forcing = (2.0 * forcing * kept_mask).astype(jnp.bfloat16)
    collected = lax.all_gather(forcing, "mode", axis=1, tiled=True)
    collected = lax.all_gather(collected, "band", axis=3, tiled=True)
    own_basis = lax.all_to_all(radiation_modes, "mode", split_axis=0, concat_axis=1, tiled=True)
    surface_force = jnp.einsum(
        "pr,wrcf->wpcf", own_basis, collected, preferred_element_type=jnp.float32
    ).astype(jnp.bfloat16)
    history = jnp.einsum(
        "wpcf,tcf->wpt", surface_force, dft_table, preferred_element_type=jnp.float32
    )
    return history.astype(jnp.bfloat16)


def solution(mesh):
    placed = (
        P(None, ("band", "mode"), None),
        P("band", "mode"),
        P("band", None, "mode"),
        P("band"),
        P(),
    )
    nb, nm = mesh.shape["band"], mesh.shape["mode"]

    def body(velocity, radiation_modes, resistance, mode_ranks, freq_table):
        windows, patches, steps = velocity.shape
        mode_cols = radiation_modes.shape[1]
        cols = 2 * (freq_table.shape[0] // nb)
        tiled = (
            windows == 1 and nm == 4 and nb == 8 and cols == 128 and mode_cols % 128 == 0
            and patches % 128 == 0 and steps % 128 == 0 and steps & (steps - 1) == 0
        )
        args = (velocity, radiation_modes, resistance, mode_ranks, freq_table)
        return fused(mesh, *args) if tiled else per_device(*args)

    return jax.shard_map(
        body,
        mesh=mesh,
        in_specs=placed,
        out_specs=P(None, ("band", "mode"), None),
        check_vma=False,
    )
```
